32 devices in a mesh: ctx: 8 (over z, y), fsdp: 4 (over x, core).
Axes of the slice: x: 2, y: 2, z: 4, core: 2. Of those that a mesh axis runs over, the one named last changes fastest.
Arguments:
- layer_input: bfloat16 [16, 8, 2, 32, 1536], P('fsdp', 'ctx'), may hold values from -6 to 6
- gain_attn: bfloat16 [1536], P('fsdp'), may hold values from 0.5 to 1.5
- w_query: bfloat16 [1536, 1536], P('fsdp'), may hold values from -0.15625 to 0.15625
- key_projection_weight: bfloat16 [1536, 512], P('fsdp'), may hold values from -0.15625 to 0.15625
- value_projection_weight: bfloat16 [1536, 512], P('fsdp'), may hold values from -0.15625 to 0.15625
- w_out: bfloat16 [1536, 1536], P('fsdp'), may hold values from -0.4375 to 0.4375
- gain_ffn: bfloat16 [1536], P('fsdp'), may hold values from 0.5 to 1.5
- w_router: bfloat16 [1536, 40], P('fsdp'), may hold values from -0.3125 to 0.3125
- w_gate: bfloat16 [40, 1536, 512], P(None, None, 'fsdp'), may hold values from -0.15625 to 0.15625
- w_up: bfloat16 [40, 1536, 512], P(None, None, 'fsdp'), may hold values from -0.15625 to 0.15625
- w_down: bfloat16 [40, 1536, 512], P(None, None, 'fsdp'), may hold values from -1 to 1
- routes: int32 [16, 8, 2, 32, 8], P(None, 'ctx'), may hold values from 0 to 39, all different within a row; in each aligned block of 64 rows (0 to 63, 64 to 127, ..., all dimensions but the last counted through in order) at most 17 rows name the same one
- lengths: int32 [16], replicated, may hold values from 128 to 512, as said below
- cotangent: bfloat16 [16, 8, 2, 32, 1536], P('fsdp', 'ctx'), may hold values from -6 to 6
Outputs:
- layer_output: bfloat16 [16, 8, 2, 32, 1536], P('fsdp', 'ctx')
- grad_input: float32 [16, 8, 2, 32, 1536], P('fsdp', 'ctx')
- grad_gain_attn: float32 [1536], P(('ctx', 'fsdp'))
- grad_w_query: float32 [1536, 1536], P(('ctx', 'fsdp'))
- grad_w_key: float32 [1536, 512], P(('ctx', 'fsdp'))
- grad_w_value: float32 [1536, 512], P(('ctx', 'fsdp'))
- grad_w_out: float32 [1536, 1536], P(('ctx', 'fsdp'))
- grad_gain_ffn: float32 [1536], P(('ctx', 'fsdp'))
- grad_w_router: float32 [1536, 40], P(('ctx', 'fsdp'))
- grad_w_gate: float32 [40, 1536, 512], P(None, 'ctx', 'fsdp')
- grad_w_up: float32 [40, 1536, 512], P(None, 'ctx', 'fsdp')
- grad_w_down: float32 [40, 1536, 512], P(None, 'ctx', 'fsdp')
- aux_loss: float32 [], replicated
The draws below stay inside these ranges and needn't reach their ends.
Inputs may be any that keep to these rules, and one draw needn't show every extreme that they name: `routes`: each slot names 8 different experts. Within one aligned block of 64 rows (the slots of one sequence on one device), no expert is named by more than 17 rows, and in every draw some expert is named by exactly 17 rows of some block. `lengths`: some sequence uses all 512 slots in every draw.
All inputs are finite; a program needn't handle non-finite values.
Results may differ from the reference program's by a relative error of at most 0.02.
Values may be sent and summed in bfloat16 or wider, within the bound.
No kernel may reach another device: no remote copies, remote signals or barrier semaphores. Data moves between devices by JAX's collectives and lax.ppermute only.
A program may use at most 448 MiB of HBM per device.

```python
import math
import jax
import jax.numpy as jnp
import numpy as np
from jax import lax

MODEL_DIM = 1536
QUERY_HEADS = 24
KEY_VALUE_HEADS = 8
HEAD_DIM = 64
E = 40
H = 512
TOP = 8
TOK_DEV = 256
SEQ_SHARE = 4
SEQUENCE_TOTAL = 16
SEQUENCE_SLOTS = 512
HALF = 32
MOST = 17
N_CTX = 8


def draw_lengths(key, part):
    group_count = SEQUENCE_TOTAL // SEQ_SHARE
    low_len = SEQUENCE_SLOTS // 4
    band = (SEQUENCE_SLOTS - low_len) // group_count
    group_ids = jnp.arange(SEQUENCE_TOTAL, dtype=jnp.int32) // SEQ_SHARE
    offsets = jax.random.randint(jax.random.fold_in(key, 11), (SEQUENCE_TOTAL,), 0, band + 1)
    drawn_len = low_len + group_ids * band + offsets
    drawn_len = jnp.minimum(drawn_len, SEQUENCE_SLOTS)
    return jnp.where(jnp.arange(SEQUENCE_TOTAL) == SEQUENCE_TOTAL - 1, SEQUENCE_SLOTS, drawn_len).astype(jnp.int32)


def with_spikes(drawn, own_key, source, target, shards_of, factor):
    owner, partner = [(jnp.arange(drawn.shape[axis_at]) // (drawn.shape[axis_at] // shards_of)).reshape([-1 if axis == axis_at else 1 for axis in range(drawn.ndim)]) for axis_at in (source, target)]
    chosen = jax.random.permutation(own_key, shards_of)[partner]
    strong = (owner == chosen) | (owner == (partner + shards_of // 2) % shards_of)
    return jnp.where(strong, factor * drawn, drawn)


def shard_levels(own_key, extent, split, least, top_value):
    def one(axis_at, shards_of):
        steps = jax.random.uniform(jax.random.fold_in(jax.random.fold_in(own_key, 6), axis_at), (shards_of,), jnp.float32, least / len(split), top_value / len(split))
        return jnp.repeat(jnp.exp(steps), extent[axis_at] // shards_of).reshape((-1,) + (1,) * (len(extent) - axis_at - 1))

    level = one(*split[0])
    for cut in split[1:]:
        level = level * one(*cut)
    return level


def routed_block(own_key, own, number, rows, count, top, most, skew):
    order = jax.random.permutation(own_key, count)
    crowded, common = portions_of(count, rows * top, most, skew, True), portions_of(count, rows * top, most, skew, False)
    places = jnp.arange(count)

    def named(sizes, offset_by):
        used = int((sizes > 0).sum())
        fixed = max(1, used // 4)
        passed = fixed + (places - fixed + offset_by * (used - fixed)) % max(1, count - fixed)
        return jnp.zeros((count,), jnp.int32).at[order[jnp.where(places < fixed, places, passed)]].set(jnp.asarray(sizes, jnp.int32))

    sizes = jnp.where(number % 4 == 0, named(crowded, number // 4), named(common, number - number // 4 - 1))
    mixed = jax.random.permutation(jax.random.fold_in(own, 3), count)
    donor, sink = mixed[0:count // 2 * 2:2], mixed[1:count // 2 * 2:2]
    margin = jnp.minimum(sizes[donor] - 1, most - sizes[sink]) // 2
    margin = jnp.where((donor == order[0]) | (sink == order[0]) | (sizes[sink] == 0), 0, jnp.maximum(margin, 0))
    passed = jax.random.randint(jax.random.fold_in(own, 4), (count // 2,), 0, 1 << 20) % (margin + 1)
    sizes = sizes.at[donor].add(-passed).at[sink].add(passed)
    members = jnp.searchsorted(jnp.cumsum(sizes), jnp.arange(rows * top), side="right").astype(jnp.int32)
    table = members.reshape(top, rows).T
    table = table[jax.random.permutation(jax.random.fold_in(own, 1), rows)]
    offset_by = jax.random.randint(jax.random.fold_in(own, 2), (rows, 1), 0, top)
    return jnp.take_along_axis(table, (jnp.arange(top)[None, :] + offset_by) % top, axis=1)


def portions_of(amount, total, bound, slope, full):
    weights = [(1 << 20) // math.isqrt(standing ** slope) + 1 for standing in range(1, amount + 1)]
    largest = bound if full else min(bound, max(-(-total // amount), total * weights[0] // sum(weights)))
    least = 1 if total - largest >= amount - 1 else 0
    given, surplus = [largest] + [least] * (amount - 1), total - largest - least * (amount - 1)
    while surplus > 0:
        candidates = [i for i in range(1, amount) if given[i] < largest] or [i for i in range(1, amount) if given[i] < bound]
        mass, budget = sum([weights[i] for i in candidates]), surplus
        for i in candidates:
            extra = min(bound - given[i], max(1, budget * weights[i] // mass), surplus)
            given[i] = given[i] + extra
            surplus = surplus - extra
    return np.array(given)


def noise(stream_key, extent, spread, reach, split=(), kind=jnp.bfloat16):
    entries = jax.random.normal(stream_key, extent, jnp.float32) * spread
    if len(split) > 0:
        entries = shard_levels(stream_key, extent, split, -0.22, 0.18) * entries
    return jnp.clip(entries, min=-reach, max=reach).astype(kind)


def heavy_noise(rng, dims, scale, most, cuts, heavy, kind=jnp.bfloat16):
    drawn = scale * jax.random.normal(rng, dims, jnp.float32)
    if cuts:
        drawn = drawn * shard_levels(rng, dims, cuts, -0.22, 0.18)
    return jnp.clip(with_spikes(drawn, jax.random.fold_in(rng, 3), *heavy), -most, most).astype(kind)


def setup_inputs(seed: int = 0) -> dict:
    arg_keys = jax.random.split(jax.random.key(seed), 15)
    layer_input = noise(arg_keys[0], (SEQUENCE_TOTAL, N_CTX, 2, HALF, MODEL_DIM), 1.0, 6.0, ((0, 4), (1, 8)))
    gain_attn = jnp.clip(1.0 + 0.1 * jax.random.normal(arg_keys[1], (MODEL_DIM,), jnp.float32), 0.5, 1.5).astype(jnp.bfloat16)
    w_query = noise(arg_keys[2], (MODEL_DIM, QUERY_HEADS * HEAD_DIM), MODEL_DIM ** -0.5, 0.15625, ((0, 4),))
    key_projection_weight = noise(arg_keys[3], (MODEL_DIM, KEY_VALUE_HEADS * HEAD_DIM), MODEL_DIM ** -0.5, 0.15625, ((0, 4),))
    value_projection_weight = noise(arg_keys[4], (MODEL_DIM, KEY_VALUE_HEADS * HEAD_DIM), MODEL_DIM ** -0.5, 0.15625, ((0, 4),))
    w_out = noise(arg_keys[5], (QUERY_HEADS * HEAD_DIM, MODEL_DIM), (max(1, QUERY_HEADS * HEAD_DIM * 64 // SEQUENCE_SLOTS)) ** -0.5, 0.4375, ((0, 4),))
    gain_ffn = jnp.clip(1.0 + 0.1 * jax.random.normal(arg_keys[6], (MODEL_DIM,), jnp.float32), 0.5, 1.5).astype(jnp.bfloat16)
    w_router = noise(arg_keys[7], (MODEL_DIM, E), (MODEL_DIM // 4) ** -0.5, 0.3125, ((0, 4),))
    w_gate = noise(arg_keys[8], (E, MODEL_DIM, H), MODEL_DIM ** -0.5, 0.15625, ((2, 4),))
    w_up = noise(arg_keys[9], (E, MODEL_DIM, H), MODEL_DIM ** -0.5, 0.15625, ((2, 4),))
    w_down = noise(arg_keys[10], (E, MODEL_DIM, H), (H // 16) ** -0.5, 1.0, ((2, 4),))
    routes_keys = jax.random.split(jax.random.fold_in(arg_keys[11], 1), SEQUENCE_TOTAL * N_CTX * 2 * HALF // (TOK_DEV // SEQ_SHARE))
    routes_turns = jax.random.permutation(jax.random.fold_in(arg_keys[11], 3), SEQUENCE_TOTAL * N_CTX * 2 * HALF // (TOK_DEV // SEQ_SHARE))
    routes = jax.vmap(lambda own, number: routed_block(jax.random.fold_in(arg_keys[11], 2), own, number, TOK_DEV // SEQ_SHARE, E, TOP, MOST, 1))(routes_keys, routes_turns).reshape((SEQUENCE_TOTAL, N_CTX, 2, HALF, TOP))
    lengths = draw_lengths(jax.random.fold_in(arg_keys[14], 71), 0)
    cotangent = heavy_noise(arg_keys[13], (SEQUENCE_TOTAL, N_CTX, 2, HALF, MODEL_DIM), 1.0, 6.0, ((0, 4), (1, 8)), (1, 4, 8, 2.0))
    return {"layer_input": layer_input, "gain_attn": gain_attn, "w_query": w_query, "key_projection_weight": key_projection_weight, "value_projection_weight": value_projection_weight, "w_out": w_out, "gain_ffn": gain_ffn, "w_router": w_router, "w_gate": w_gate, "w_up": w_up, "w_down": w_down, "routes": routes, "lengths": lengths, "cotangent": cotangent}


@jax.custom_vjp
def reduced_precision(v):
    return lax.optimization_barrier(v.astype(jnp.bfloat16)).astype(jnp.float32)

@jax.custom_vjp
def reduced_backward(v):
    return v

def low_keep(v):
    return (reduced_precision(v), None)

def low_pass(kept, grad):
    return (grad,)

def back_keep(v):
    return (v, None)

def back_low(kept, grad):
    return (reduced_precision(grad),)
reduced_precision.defvjp(low_keep, low_pass)
reduced_backward.defvjp(back_keep, back_low)
epsilon = 1e-05
rope_base = 10000.0
loss_weight = 0.01
highest = lax.Precision.HIGHEST

def matrix_product(pattern, left_side, right_side):
    return jnp.einsum(pattern, left_side, right_side, precision=highest)

def rms_scale(values):
    return lax.rsqrt(lax.optimization_barrier(jnp.mean(values * values, -1, keepdims=True)) + epsilon)

def apply_rotation(values, token_positions):
    frequency = rope_base ** (-jnp.arange(HEAD_DIM // 2, dtype=jnp.float32) * 2.0 / HEAD_DIM)
    angles = token_positions.astype(jnp.float32)[..., None] * frequency
    cosine = jnp.cos(angles)[..., None, :]
    sine_part = jnp.sin(angles)[..., None, :]
    first_half = values[..., :HEAD_DIM // 2]
    second = values[..., HEAD_DIM // 2:]
    return jnp.concatenate([first_half * cosine - second * sine_part, second * cosine + first_half * sine_part], -1)

def attend_sequence(query_rows, key_entries, value_entries, length):
    query_tile_rows = min(512, SEQUENCE_SLOTS)
    block_tally = SEQUENCE_SLOTS // query_tile_rows
    start_offsets = jnp.arange(block_tally, dtype=jnp.int32) * query_tile_rows
    query_tile_list = query_rows.reshape(block_tally, query_tile_rows, KEY_VALUE_HEADS, QUERY_HEADS // KEY_VALUE_HEADS, HEAD_DIM)
    key_pos = jnp.arange(SEQUENCE_SLOTS, dtype=jnp.int32)

    @jax.checkpoint
    def single_block(pieces):
        query_part, first_row = pieces
        raw_scores = reduced_backward(matrix_product('qhgd,khd->hgqk', query_part, key_entries)) * HEAD_DIM ** (-0.5)
        query_pos = first_row + jnp.arange(query_tile_rows, dtype=jnp.int32)
        visible = (key_pos[None, :] <= query_pos[:, None]) & (key_pos[None, :] < length)
        scores = jnp.where(visible, raw_scores, -1e+30)
        soft_prob = jax.nn.softmax(scores, axis=-1)
        return matrix_product('hgqk,khd->qhgd', reduced_precision(soft_prob), value_entries)
    return lax.map(single_block, (query_tile_list, start_offsets)).reshape(SEQUENCE_SLOTS, KEY_VALUE_HEADS, QUERY_HEADS // KEY_VALUE_HEADS, HEAD_DIM)

def reference(layer_input, gain_attn, w_query, key_projection_weight, value_projection_weight, w_out, gain_ffn, w_router, w_gate, w_up, w_down, routes, lengths, cotangent):
    query_group_width = QUERY_HEADS // KEY_VALUE_HEADS
    block_count = SEQUENCE_TOTAL * N_CTX
    block_rows = TOK_DEV // SEQ_SHARE
    dev_ids = jnp.arange(N_CTX, dtype=jnp.int32)[:, None, None]
    half_ids = jnp.arange(2, dtype=jnp.int32)[None, :, None]
    row_ids = jnp.arange(HALF, dtype=jnp.int32)[None, None, :]
    token_positions = (jnp.where(half_ids == 0, dev_ids, 2 * N_CTX - 1 - dev_ids) * HALF + row_ids).reshape(SEQUENCE_SLOTS)
    sorted_order = jnp.argsort(token_positions).astype(jnp.int32)
    live_rows = (token_positions[None, :] < lengths[:, None]).astype(jnp.float32)
    route_pairs = routes.reshape(block_count, block_rows * TOP)
    pair_hot = (route_pairs[..., None] == jnp.arange(E, dtype=jnp.int32)).astype(jnp.int32)
    rank_pair = lax.optimization_barrier(jnp.sum((jnp.cumsum(pair_hot, axis=1) - 1) * pair_hot, -1)).astype(jnp.int32)
    slot_ids = (route_pairs * MOST + rank_pair).astype(jnp.int32)
    block_ids = jnp.broadcast_to(jnp.arange(block_count, dtype=jnp.int32)[:, None], slot_ids.shape)
    pair_ids = jnp.broadcast_to(jnp.arange(block_rows * TOP, dtype=jnp.int32)[None, :], slot_ids.shape)
    slot_table = jnp.full((block_count, E * MOST), -1, jnp.int32).at[block_ids, slot_ids].set(pair_ids)
    slot_table = slot_table.reshape(block_count, E, MOST)
    counts = lax.optimization_barrier(jnp.sum(lax.optimization_barrier(jnp.sum(pair_hot.reshape(SEQUENCE_TOTAL, SEQUENCE_SLOTS, TOP, E), 2)).astype(jnp.float32) * live_rows[..., None], (0, 1)))
    live_total = jnp.sum(live_rows)
    route_share = counts / (TOP * live_total)

    def attend_one(pieces):
        return attend_sequence(pieces[0], pieces[1], pieces[2], pieces[3])

    def forward(params, inputs):
        gain_one, query_matrix, key_matrix, value_matrix, output_matrix, gain_two, router_matrix, gate_w, up_w, down_w = params
        rows_in = inputs.reshape(SEQUENCE_TOTAL, SEQUENCE_SLOTS, MODEL_DIM)
        unit_one = rows_in * rms_scale(rows_in)
        first_normed = reduced_precision(unit_one * gain_one)
        query_unrotated = reduced_backward(matrix_product('zig,gx->zix', first_normed, query_matrix))
        key_unrotated = reduced_backward(matrix_product('zig,gx->zix', first_normed, key_matrix))
        value_entries = reduced_precision(reduced_backward(matrix_product('zig,gx->zix', first_normed, value_matrix)))
        query_rows = reduced_precision(apply_rotation(query_unrotated.reshape(SEQUENCE_TOTAL, SEQUENCE_SLOTS, QUERY_HEADS, HEAD_DIM), token_positions))
        key_entries = reduced_precision(apply_rotation(key_unrotated.reshape(SEQUENCE_TOTAL, SEQUENCE_SLOTS, KEY_VALUE_HEADS, HEAD_DIM), token_positions))
        value_entries = value_entries.reshape(SEQUENCE_TOTAL, SEQUENCE_SLOTS, KEY_VALUE_HEADS, HEAD_DIM)
        query_rows = query_rows[:, sorted_order].reshape(SEQUENCE_TOTAL, SEQUENCE_SLOTS, KEY_VALUE_HEADS, query_group_width, HEAD_DIM)
        key_entries = key_entries[:, sorted_order]
        value_entries = value_entries[:, sorted_order]
        attended = lax.map(attend_one, (query_rows, key_entries, value_entries, lengths))
        attended = attended.reshape(SEQUENCE_TOTAL, SEQUENCE_SLOTS, QUERY_HEADS * HEAD_DIM)[:, token_positions]
        mixed_attention = reduced_precision(reduced_backward(attended))
        branch_output = reduced_backward(matrix_product('gay,yv->gav', mixed_attention, output_matrix))
        residual = rows_in + branch_output
        unit_two = residual * rms_scale(residual)
        second_normed = reduced_precision(unit_two * gain_two)
        router_logits = reduced_backward(matrix_product('zig,gx->zix', second_normed, router_matrix))
        router_probs = jax.nn.softmax(router_logits, axis=-1)
        route_gates = jnp.take_along_axis(router_probs.reshape(block_count, block_rows, E), routes.reshape(block_count, block_rows, TOP), axis=-1)

        @jax.checkpoint
        def expert_block(pieces):
            block_in, block_gates, block_table = pieces
            live_slot = block_table >= 0
            pair_id = jnp.maximum(block_table, 0)
            token_id = pair_id // TOP
            picked = block_in[token_id]
            slot_gate = jnp.where(live_slot, block_gates.reshape(-1)[pair_id], 0.0)
            gate_pre = reduced_backward(matrix_product('emd,edh->emh', picked, gate_w))
            up_pre = reduced_backward(matrix_product('emd,edh->emh', picked, up_w))
            scaled = reduced_precision(slot_gate[..., None] * jax.nn.silu(gate_pre) * up_pre)
            produced = matrix_product('emh,edh->emd', scaled, down_w)
            return jnp.zeros((block_rows, MODEL_DIM), jnp.float32).at[token_id.reshape(-1)].add(produced.reshape(-1, MODEL_DIM))
        moe = lax.map(expert_block, (second_normed.reshape(block_count, block_rows, MODEL_DIM), route_gates, slot_table))
        moe = reduced_backward(moe.reshape(SEQUENCE_TOTAL, SEQUENCE_SLOTS, MODEL_DIM))
        block_out = residual + moe
        prob_mass = lax.optimization_barrier(jnp.sum(router_probs * live_rows[..., None], (0, 1)))
        aux_loss = E * jnp.sum(route_share * prob_mass / live_total)
        return (block_out.reshape(inputs.shape), aux_loss)
    params = (gain_attn.astype(jnp.float32), w_query.astype(jnp.float32), key_projection_weight.astype(jnp.float32), value_projection_weight.astype(jnp.float32), w_out.astype(jnp.float32), gain_ffn.astype(jnp.float32), w_router.astype(jnp.float32), w_gate.astype(jnp.float32), w_up.astype(jnp.float32), w_down.astype(jnp.float32))
    inputs = layer_input.astype(jnp.float32)
    (block_out, aux_loss), pullback = jax.vjp(forward, params, inputs)
    live_slots = live_rows.reshape(SEQUENCE_TOTAL, N_CTX, 2, HALF)[..., None]
    cot_rows = cotangent.astype(jnp.float32) * live_slots
    grad_params, grad_input = pullback((cot_rows, jnp.asarray(loss_weight, dtype=jnp.float32)))
    return (block_out.astype(jnp.bfloat16), grad_input, grad_params[0], grad_params[1], grad_params[2], grad_params[3], grad_params[4], grad_params[5], grad_params[6], grad_params[7], grad_params[8], grad_params[9], aux_loss)
```

```python
import jax
import jax.numpy as jnp
from jax import lax
from jax.experimental import pallas as pl
from jax.experimental.pallas import tpu as pltpu
from jax.sharding import PartitionSpec as P

QUERY_HEADS = 24
KEY_VALUE_HEADS = 8
HEAD_DIM = 64
LANES = 128
EXPERT_CALLS = 4
ROW_BLOCK = 256


epsilon = 1e-05
rope_base = 10000.0
loss_weight = 0.01
mask_value = -1e30


def rms_scale(values):
    return lax.rsqrt(jnp.mean(values * values, -1, keepdims=True) + epsilon)


def rope_tables(token_positions):
    frequency = rope_base ** (-jnp.arange(HEAD_DIM // 2, dtype=jnp.float32) * 2.0 / HEAD_DIM)
    angles = token_positions.astype(jnp.float32)[..., None] * frequency
    return (jnp.cos(angles)[..., None, :], jnp.sin(angles)[..., None, :])


def apply_rotation(values, token_positions):
    cosine, sine_part = rope_tables(token_positions)
    first_half = values[..., : HEAD_DIM // 2]
    second = values[..., HEAD_DIM // 2 :]
    return jnp.concatenate(
        [first_half * cosine - second * sine_part, second * cosine + first_half * sine_part], -1
    )


def unrotate(gradient, token_positions):
    cosine, sine_part = rope_tables(token_positions)
    first_half = gradient[..., : HEAD_DIM // 2]
    second = gradient[..., HEAD_DIM // 2 :]
    return jnp.concatenate(
        [first_half * cosine + second * sine_part, second * cosine - first_half * sine_part], -1
    )


def inner_rows(left_side, right_side):
    return lax.dot_general(
        left_side, right_side, (((0,), (0,)), ((), ())), preferred_element_type=jnp.float32
    )


def back_rows(gradient, weight):
    return lax.dot_general(
        gradient, weight, (((1,), (1,)), ((), ())), preferred_element_type=jnp.float32
    )


def gathered_positions(key_index, sequence_rows, half_rows, n_ctx):
    device = key_index // sequence_rows
    within = key_index % sequence_rows
    block_id = jnp.where(within < half_rows, device, 2 * n_ctx - 1 - device)
    return block_id * half_rows + within % half_rows


def block_scores(query_rotated_rows, key_portion, query_pos, key_pos, key_live):
    raw_scores = jnp.einsum(
        "sqhgd,kshd->shgqk", query_rotated_rows, key_portion, preferred_element_type=jnp.float32
    ) * HEAD_DIM ** (-0.5)
    causal = key_pos[None, :] <= query_pos[:, None]
    visible = (causal[None] & key_live.T[:, None, :])[:, None, None]
    return (jnp.where(visible, raw_scores, mask_value), visible)


def expert_call(
    first_expert,
    expert_total,
    normed_rows,
    normed_turned,
    cotangent_rows,
    cotangent_turned,
    gate_table,
    w_gate,
    w_up,
    w_down,
):
    rows, width = normed_rows.shape
    hidden = w_gate.shape[2]
    pair_width = 2 * hidden
    width_block = width // 3

    def kernel(
        normed,
        normed_t,
        cotan,
        cotan_t,
        gates,
        gate_w,
        up_w,
        down_w,
        gate_grad,
        up_grad,
        down_grad,
        moe,
        d_rows,
        d_gates,
        scaled_keep,
        d_gate_keep,
        d_up_keep,
    ):
        pair = pl.program_id(0)
        first = first_expert + 2 * pair

        @pl.when(pair == 0)
        def _():
            moe[...] = jnp.zeros_like(moe)
            d_rows[...] = jnp.zeros_like(d_rows)
            d_gates[...] = jnp.zeros_like(d_gates)

        def joined(pair_ref):
            return jnp.concatenate([pair_ref[0], pair_ref[1]], axis=1)

        def plain(left_side, right_side):
            return jnp.dot(left_side, right_side, preferred_element_type=jnp.float32)

        def turned(left_side, right_side):
            return lax.dot_general(
                left_side, right_side, (((1,), (1,)), ((), ())), preferred_element_type=jnp.float32
            )

        gate_pair, up_pair, down_pair = joined(gate_w), joined(up_w), joined(down_w)
        lane = lax.broadcasted_iota(jnp.int32, (ROW_BLOCK, LANES), 1)

        def row_step(block, carry):
            span = pl.ds(pl.multiple_of(block * ROW_BLOCK, ROW_BLOCK), ROW_BLOCK)
            normed_part, cotan_part = normed[span, :], cotan[span, :]
            gate_part = gates[span, :]
            slot_gate = jnp.concatenate(
                [
                    jnp.broadcast_to(
                        jnp.sum(
                            jnp.where(lane == first + j, gate_part, 0.0), axis=1, keepdims=True
                        ),
                        (ROW_BLOCK, hidden),
                    )
                    for j in range(2)
                ],
                axis=1,
            )
            gate_pre = plain(normed_part, gate_pair)
            up_pre = plain(normed_part, up_pair)
            d_scaled = plain(cotan_part, down_pair)
            sigmoid_gate = jax.nn.sigmoid(gate_pre)
            silu_gate = gate_pre * sigmoid_gate
            scaled = (slot_gate * silu_gate * up_pre).astype(jnp.bfloat16)
            gate_term = d_scaled * silu_gate * up_pre
            d_gate_part = d_gates[span, :]
            for j in range(2):
                d_gate_part = d_gate_part + jnp.where(
                    lane == first + j,
                    jnp.sum(gate_term[:, j * hidden : (j + 1) * hidden], axis=1, keepdims=True),
                    0.0,
                )
            d_gates[span, :] = d_gate_part
            d_act = d_scaled * slot_gate
            d_gate_pre = (
                d_act * up_pre * (sigmoid_gate + silu_gate * (1.0 - sigmoid_gate))
            ).astype(jnp.bfloat16)
            d_up_pre = (d_act * silu_gate).astype(jnp.bfloat16)
            scaled_keep[span, :] = scaled
            d_gate_keep[span, :] = d_gate_pre
            d_up_keep[span, :] = d_up_pre
            moe[span, :] += turned(scaled, down_pair)
            d_rows[span, :] += turned(d_gate_pre, gate_pair) + turned(d_up_pre, up_pair)
            return carry

        lax.fori_loop(0, rows // ROW_BLOCK, row_step, 0)

        def width_step(block, carry):
            span = pl.ds(pl.multiple_of(block * width_block, width_block), width_block)
            for source, kept, grad in (
                (normed_t, d_gate_keep, gate_grad),
                (normed_t, d_up_keep, up_grad),
                (cotan_t, scaled_keep, down_grad),
            ):
                term = plain(source[span, :], kept[...]).astype(jnp.bfloat16)
                for j in range(2):
                    grad[j, span, :] = term[:, j * hidden : (j + 1) * hidden]
            return carry

        lax.fori_loop(0, 3, width_step, 0)

    def whole(shape):
        return pl.BlockSpec(shape, lambda pair: (0, 0), pipeline_mode=pl.Buffered(1))

    def pair_block(offset):
        return pl.BlockSpec((2, width, hidden), lambda pair: (pair + offset, 0, 0))

    start = first_expert // 2
    grad_shape = jax.ShapeDtypeStruct((expert_total, width, hidden), jnp.bfloat16)
    row_shape = jax.ShapeDtypeStruct((rows, width), jnp.float32)
    outs = pl.pallas_call(
        kernel,
        grid=(expert_total // 2,),
        in_specs=[
            whole((rows, width)),
            whole((width, rows)),
            whole((rows, width)),
            whole((width, rows)),
            whole((rows, LANES)),
            pair_block(start),
            pair_block(start),
            pair_block(start),
        ],
        out_specs=[pair_block(0)] * 3
        + [whole((rows, width)), whole((rows, width)), whole((rows, LANES))],
        out_shape=[grad_shape] * 3
        + [row_shape, row_shape, jax.ShapeDtypeStruct((rows, LANES), jnp.float32)],
        scratch_shapes=[pltpu.VMEM((rows, pair_width), jnp.bfloat16)] * 3,
        name="expert_step",
        compiler_params=pltpu.CompilerParams(
            dimension_semantics=("arbitrary",), vmem_limit_bytes=60 * 1024 * 1024
        ),
    )(
        normed_rows,
        normed_turned,
        cotangent_rows,
        cotangent_turned,
        gate_table,
        w_gate,
        w_up,
        w_down,
    )
    return outs[:3], outs[3], outs[4], outs[5]


def local(
    layer_input,
    gain_attn,
    w_query,
    key_projection_weight,
    value_projection_weight,
    w_out,
    gain_ffn,
    w_router,
    w_gate,
    w_up,
    w_down,
    routes,
    lengths,
    cotangent,
):
    n_ctx = lax.axis_size("ctx")
    n_shard = lax.axis_size("fsdp")
    ctx_pos = lax.axis_index("ctx")
    shard_pos = lax.axis_index("fsdp")
    local_sequences = layer_input.shape[0]
    half_rows = layer_input.shape[3]
    model_width = layer_input.shape[4]
    sequence_rows = 2 * half_rows
    tokens = local_sequences * sequence_rows
    seq_len = n_ctx * sequence_rows
    experts = w_gate.shape[0]
    top_k = routes.shape[4]
    query_group_width = QUERY_HEADS // KEY_VALUE_HEADS
    key_value_width = KEY_VALUE_HEADS * HEAD_DIM
    key_tile_rows = min(512, seq_len)
    key_blocks = seq_len // key_tile_rows
    gathered_rows = n_shard * tokens
    local_positions = gathered_positions(
        ctx_pos * sequence_rows + jnp.arange(sequence_rows, dtype=jnp.int32),
        sequence_rows,
        half_rows,
        n_ctx,
    )
    seq_lengths = lax.dynamic_slice_in_dim(lengths, shard_pos * local_sequences, local_sequences)
    live_rows = (
        (local_positions[None, :] < seq_lengths[:, None]).astype(jnp.float32).reshape(tokens)
    )
    gain_one, query_matrix, key_matrix, value_matrix, output_matrix, gain_two, router_matrix = (
        lax.all_gather(gain_attn, "fsdp", axis=0, tiled=True),
        lax.all_gather(w_query, "fsdp", axis=0, tiled=True),
        lax.all_gather(key_projection_weight, "fsdp", axis=0, tiled=True),
        lax.all_gather(value_projection_weight, "fsdp", axis=0, tiled=True),
        lax.all_gather(w_out, "fsdp", axis=0, tiled=True),
        lax.all_gather(gain_ffn, "fsdp", axis=0, tiled=True),
        lax.all_gather(w_router, "fsdp", axis=0, tiled=True),
    )
    d_final = cotangent.reshape(tokens, model_width).astype(jnp.float32) * live_rows[:, None]
    d_moe_all = lax.all_gather(d_final.astype(jnp.bfloat16), "fsdp", axis=0, tiled=True)
    input_rows = layer_input.reshape(tokens, model_width).astype(jnp.float32)
    scale_one = rms_scale(input_rows)
    unit_one = input_rows * scale_one
    first_normed = (unit_one * gain_one.astype(jnp.float32)).astype(jnp.bfloat16)
    normed_seq = first_normed.reshape(local_sequences, sequence_rows, model_width)
    query_unrotated = jnp.dot(first_normed, query_matrix, preferred_element_type=jnp.float32)
    key_unrotated = jnp.einsum(
        "std,df->tsf", normed_seq, key_matrix, preferred_element_type=jnp.float32
    )
    value_pre = jnp.einsum(
        "std,df->tsf", normed_seq, value_matrix, preferred_element_type=jnp.float32
    )
    query_rotated_rows = apply_rotation(
        query_unrotated.reshape(local_sequences, sequence_rows, QUERY_HEADS, HEAD_DIM),
        local_positions,
    ).astype(jnp.bfloat16)
    query_rotated_rows = query_rotated_rows.reshape(
        local_sequences, sequence_rows, KEY_VALUE_HEADS, query_group_width, HEAD_DIM
    )
    key_rotated_rows = apply_rotation(
        key_unrotated.reshape(sequence_rows, local_sequences, KEY_VALUE_HEADS, HEAD_DIM),
        local_positions[:, None],
    ).astype(jnp.bfloat16)
    key_rotated_rows = key_rotated_rows.reshape(sequence_rows, local_sequences, key_value_width)
    value_low = value_pre.astype(jnp.bfloat16)
    key_all, value_all = (
        lax.all_gather(key_rotated_rows, "ctx", axis=0, tiled=True),
        lax.all_gather(value_low, "ctx", axis=0, tiled=True),
    )

    def key_info(block_id):
        key_index = block_id * key_tile_rows + jnp.arange(key_tile_rows, dtype=jnp.int32)
        key_pos = gathered_positions(key_index, sequence_rows, half_rows, n_ctx)
        return (key_pos, key_pos[:, None] < seq_lengths[None, :])

    def key_slices(key_src, value_src, block_id):
        key_portion = lax.dynamic_slice_in_dim(key_src, block_id * key_tile_rows, key_tile_rows, 0)
        value_portion = lax.dynamic_slice_in_dim(
            value_src, block_id * key_tile_rows, key_tile_rows, 0
        )
        return (
            key_portion.reshape(key_tile_rows, local_sequences, KEY_VALUE_HEADS, HEAD_DIM),
            value_portion.reshape(key_tile_rows, local_sequences, KEY_VALUE_HEADS, HEAD_DIM),
        )

    def running_max(state_pair, block_id):
        top_score, row_total = state_pair
        key_pos, key_live = key_info(block_id)
        key_portion, value_portion = key_slices(key_all, value_all, block_id)
        scores, visible = block_scores(
            query_rotated_rows, key_portion, local_positions, key_pos, key_live
        )
        new_top = jnp.maximum(top_score, jnp.max(scores, -1))
        row_total = row_total * jnp.exp(top_score - new_top) + jnp.sum(
            jnp.where(visible, jnp.exp(scores - new_top[..., None]), 0.0), -1
        )
        return ((new_top, row_total), None)

    statistic_shape = (local_sequences, KEY_VALUE_HEADS, query_group_width, sequence_rows)
    lse_pair, unused = lax.scan(
        running_max,
        (
            jnp.full(statistic_shape, mask_value, jnp.float32),
            jnp.zeros(statistic_shape, jnp.float32),
        ),
        jnp.arange(key_blocks),
    )
    log_norm = lse_pair[0] + jnp.log(lse_pair[1])

    def weigh_values(acc_out, block_id):
        key_pos, key_live = key_info(block_id)
        key_portion, value_portion = key_slices(key_all, value_all, block_id)
        scores, visible = block_scores(
            query_rotated_rows, key_portion, local_positions, key_pos, key_live
        )
        prob_low = jnp.where(visible, jnp.exp(scores - log_norm[..., None]), 0.0).astype(
            jnp.bfloat16
        )
        return (
            acc_out
            + jnp.einsum(
                "shgqk,kshd->sqhgd", prob_low, value_portion, preferred_element_type=jnp.float32
            ),
            None,
        )

    attended, unused = lax.scan(
        weigh_values,
        jnp.zeros(
            (local_sequences, sequence_rows, KEY_VALUE_HEADS, query_group_width, HEAD_DIM),
            jnp.float32,
        ),
        jnp.arange(key_blocks),
    )
    attended_low = attended.astype(jnp.bfloat16).reshape(tokens, QUERY_HEADS * HEAD_DIM)
    branch_output = jnp.dot(attended_low, output_matrix, preferred_element_type=jnp.float32)
    residual = input_rows + branch_output
    scale_two = rms_scale(residual)
    unit_two = residual * scale_two
    second_normed = (unit_two * gain_two.astype(jnp.float32)).astype(jnp.bfloat16)
    normed_all = lax.all_gather(second_normed, "fsdp", axis=0, tiled=True)
    router_logits = jnp.dot(normed_all, router_matrix, preferred_element_type=jnp.float32)
    router_probs = jax.nn.softmax(router_logits, axis=-1)
    route_rows = routes.reshape(gathered_rows, top_k)
    route_hot = jnp.any(
        route_rows[..., None] == jnp.arange(experts, dtype=jnp.int32), axis=1
    ).astype(jnp.float32)
    live_everywhere = (
        (local_positions[None, :] < lengths[:, None]).astype(jnp.float32).reshape(gathered_rows)
    )
    expert_gates = router_probs * route_hot
    gate_table = jnp.pad(expert_gates, ((0, 0), (0, LANES - experts)))
    pieces = EXPERT_CALLS
    per_call = experts // pieces
    grad_pieces, moe_pieces, row_pieces, gate_pieces = [], [], [], []
    normed_turned = normed_all.T
    d_moe_turned = d_moe_all.T
    for piece in range(pieces):
        piece_grads, moe_piece, row_piece, gate_piece = expert_call(
            piece * per_call,
            per_call,
            normed_all,
            normed_turned,
            d_moe_all,
            d_moe_turned,
            gate_table,
            w_gate,
            w_up,
            w_down,
        )
        grad_pieces.append(
            [
                lax.psum_scatter(piece_grad, "ctx", scatter_dimension=1, tiled=True).astype(
                    jnp.float32
                )
                for piece_grad in piece_grads
            ]
        )
        moe_pieces.append(moe_piece)
        row_pieces.append(row_piece)
        gate_pieces.append(gate_piece)
    grad_gate, grad_up, grad_down = (
        jnp.concatenate([grads[kind] for grads in grad_pieces], 0) for kind in range(3)
    )
    d_own = lax.psum_scatter(
        sum(row_pieces).astype(jnp.bfloat16), "fsdp", scatter_dimension=0, tiled=True
    ).astype(jnp.float32)
    d_gate_own = lax.psum_scatter(
        (sum(gate_pieces)[:, :experts] * route_hot).astype(jnp.bfloat16),
        "fsdp",
        scatter_dimension=0,
        tiled=True,
    ).astype(jnp.float32)
    moe_own = lax.psum_scatter(
        sum(moe_pieces).astype(jnp.bfloat16), "fsdp", scatter_dimension=0, tiled=True
    ).astype(jnp.float32)
    block_out = residual + moe_own
    layer_output = block_out.astype(jnp.bfloat16).reshape(layer_input.shape)
    own_probs = lax.dynamic_slice_in_dim(router_probs, shard_pos * tokens, tokens, 0)
    group_sums = jnp.concatenate(
        [
            jnp.sum(route_hot * live_everywhere[:, None], 0),
            jnp.sum(router_probs * live_everywhere[:, None], 0),
        ]
    )
    all_sums = jnp.sum(lax.all_gather(group_sums, "ctx", axis=0, tiled=False), 0)
    count_all, mass_all = all_sums[:experts], all_sums[experts:]
    live_all = jnp.sum(lengths).astype(jnp.float32)
    route_share = count_all / (top_k * live_all)
    aux_loss = experts * jnp.sum(route_share * mass_all / live_all)
    d_probs = (
        d_gate_own
        + loss_weight * experts * route_share[None, :] * live_rows[:, None] / live_all
    )
    d_logits = (own_probs * (d_probs - jnp.sum(own_probs * d_probs, -1, keepdims=True))).astype(
        jnp.bfloat16
    )
    grad_router = inner_rows(second_normed, d_logits)
    d_normed_two = d_own + back_rows(d_logits, router_matrix)
    d_unit_two = d_normed_two * gain_two.astype(jnp.float32)
    grad_gain_two = jnp.sum(d_normed_two * unit_two, 0)
    d_resid = d_final + scale_two * (
        d_unit_two - unit_two * jnp.mean(d_unit_two * unit_two, -1, keepdims=True)
    )
    d_branch = d_resid.astype(jnp.bfloat16)
    grad_out = inner_rows(attended_low, d_branch)
    early_terms = jnp.concatenate(
        [
            grad_out,
            jnp.pad(
                jnp.concatenate([grad_router, grad_gain_two[:, None]], 1),
                ((0, 0), (0, LANES - experts - 1)),
            ),
        ],
        1,
    ).astype(jnp.bfloat16)
    d_attended = (
        back_rows(d_branch, output_matrix)
        .astype(jnp.bfloat16)
        .reshape(local_sequences, sequence_rows, KEY_VALUE_HEADS, query_group_width, HEAD_DIM)
    )
    row_delta = jnp.sum(d_attended.astype(jnp.float32) * attended, -1).transpose(0, 2, 3, 1)
    key_again, value_again = (key_all, value_all)

    def attend_back(d_query, block_id):
        key_pos, key_live = key_info(block_id)
        key_portion, value_portion = key_slices(key_again, value_again, block_id)
        scores, visible = block_scores(
            query_rotated_rows, key_portion, local_positions, key_pos, key_live
        )
        soft_prob = jnp.where(visible, jnp.exp(scores - log_norm[..., None]), 0.0)
        d_value = jnp.einsum(
            "shgqk,sqhgd->kshd",
            soft_prob.astype(jnp.bfloat16),
            d_attended,
            preferred_element_type=jnp.float32,
        )
        d_prob = jnp.einsum(
            "sqhgd,kshd->shgqk", d_attended, value_portion, preferred_element_type=jnp.float32
        )
        d_score = (soft_prob * (d_prob - row_delta[..., None]) * HEAD_DIM ** (-0.5)).astype(
            jnp.bfloat16
        )
        d_query = d_query + jnp.einsum(
            "shgqk,kshd->sqhgd", d_score, key_portion, preferred_element_type=jnp.float32
        )
        d_key = jnp.einsum(
            "shgqk,sqhgd->kshd", d_score, query_rotated_rows, preferred_element_type=jnp.float32
        )
        return (
            d_query,
            (
                d_key.reshape(key_tile_rows, local_sequences, key_value_width),
                d_value.reshape(key_tile_rows, local_sequences, key_value_width),
            ),
        )

    d_query, kv_terms = lax.scan(
        attend_back,
        jnp.zeros(
            (local_sequences, sequence_rows, KEY_VALUE_HEADS, query_group_width, HEAD_DIM),
            jnp.float32,
        ),
        jnp.arange(key_blocks),
    )
    key_value_gradient = lax.psum_scatter(
        jnp.concatenate(
            [
                term.reshape(seq_len, local_sequences, key_value_width).astype(jnp.bfloat16)
                for term in kv_terms
            ],
            -1,
        ),
        "ctx",
        scatter_dimension=0,
        tiled=True,
    ).astype(jnp.float32)
    local_key_gradient = key_value_gradient[..., :key_value_width]
    d_value_own = key_value_gradient[..., key_value_width:]
    d_query_low = (
        unrotate(
            d_query.reshape(local_sequences, sequence_rows, QUERY_HEADS, HEAD_DIM), local_positions
        )
        .astype(jnp.bfloat16)
        .reshape(tokens, QUERY_HEADS * HEAD_DIM)
    )
    d_key_low = unrotate(
        local_key_gradient.reshape(sequence_rows, local_sequences, KEY_VALUE_HEADS, HEAD_DIM),
        local_positions[:, None],
    ).astype(jnp.bfloat16)
    d_key_low = d_key_low.reshape(sequence_rows, local_sequences, key_value_width)
    d_value_low = d_value_own.astype(jnp.bfloat16)
    grad_query = inner_rows(first_normed, d_query_low)
    grad_key = jnp.einsum("std,tsf->df", normed_seq, d_key_low, preferred_element_type=jnp.float32)
    grad_value = jnp.einsum(
        "std,tsf->df", normed_seq, d_value_low, preferred_element_type=jnp.float32
    )
    d_normed_one = (
        back_rows(d_query_low, query_matrix)
        + jnp.einsum(
            "tsf,df->std", d_key_low, key_matrix, preferred_element_type=jnp.float32
        ).reshape(tokens, model_width)
        + jnp.einsum(
            "tsf,df->std", d_value_low, value_matrix, preferred_element_type=jnp.float32
        ).reshape(tokens, model_width)
    )
    d_unit_one = d_normed_one * gain_one.astype(jnp.float32)
    grad_gain_one = jnp.sum(d_normed_one * unit_one, 0)
    grad_input = d_resid + scale_one * (
        d_unit_one - unit_one * jnp.mean(d_unit_one * unit_one, -1, keepdims=True)
    )
    late_rows = lax.psum_scatter(
        jnp.concatenate(
            [grad_query, grad_key, grad_value, jnp.pad(grad_gain_one[:, None], ((0, 0), (0, 127)))],
            1,
        ).astype(jnp.bfloat16),
        ("ctx", "fsdp"),
        scatter_dimension=0,
        tiled=True,
    ).astype(jnp.float32)
    early_rows = lax.psum_scatter(early_terms, ("ctx", "fsdp"), scatter_dimension=0, tiled=True)
    early_rows = early_rows.astype(jnp.float32)
    query_width = QUERY_HEADS * HEAD_DIM
    key_end = query_width + key_value_width
    value_end = key_end + key_value_width
    summed = (
        late_rows[:, value_end],
        late_rows[:, :query_width],
        late_rows[:, query_width:key_end],
        late_rows[:, key_end:value_end],
        early_rows[:, :model_width],
        early_rows[:, model_width + experts],
        early_rows[:, model_width : model_width + experts],
    )
    return (
        layer_output,
        grad_input.reshape(layer_input.shape),
        summed[0],
        summed[1],
        summed[2],
        summed[3],
        summed[4],
        summed[5],
        summed[6],
        grad_gate,
        grad_up,
        grad_down,
        aux_loss,
    )


def solution(mesh):
    placed = (
        P("fsdp", "ctx", None, None, None),
        P("fsdp"),
        P("fsdp", None),
        P("fsdp", None),
        P("fsdp", None),
        P("fsdp", None),
        P("fsdp"),
        P("fsdp", None),
        P(None, None, "fsdp"),
        P(None, None, "fsdp"),
        P(None, None, "fsdp"),
        P(None, "ctx", None, None, None),
        P(),
        P("fsdp", "ctx", None, None, None),
    )
    return jax.shard_map(
        local,
        mesh=mesh,
        in_specs=placed,
        out_specs=(
            P("fsdp", "ctx", None, None, None),
            P("fsdp", "ctx", None, None, None),
            P(("ctx", "fsdp")),
            P(("ctx", "fsdp"), None),
            P(("ctx", "fsdp"), None),
            P(("ctx", "fsdp"), None),
            P(("ctx", "fsdp"), None),
            P(("ctx", "fsdp")),
            P(("ctx", "fsdp"), None),
            P(None, "ctx", "fsdp"),
            P(None, "ctx", "fsdp"),
            P(None, "ctx", "fsdp"),
            P(),
        ),
        check_vma=False,
    )
```

```python
import jax
import jax.numpy as jnp
from jax import lax
from jax.experimental import pallas as pl
from jax.experimental.pallas import tpu as pltpu
from jax.sharding import Mesh
from jax.sharding import PartitionSpec as P

QUERY_HEADS = 24
KEY_VALUE_HEADS = 8
HEAD_DIM = 64
GROUP = QUERY_HEADS // KEY_VALUE_HEADS
QUERY_GROUP = GROUP * HEAD_DIM
FUSED_GROUP = QUERY_GROUP + 2 * HEAD_DIM
FUSED_WIDTH = KEY_VALUE_HEADS * FUSED_GROUP
LANES = 128
ROW_BLOCK = 512
CHUNKS = (8, 8, 8, 8, 8)
CTX = ("z", "y")
SHARD = ("x", "k")
EVERY = ("z", "y", "x", "k")

epsilon = 1e-05
rope_base = 10000.0
loss_weight = 0.01
mask_value = -1e30


def plain(left_side, right_side):
    return jnp.dot(left_side, right_side, preferred_element_type=jnp.float32)


def turned(left_side, right_side):
    return lax.dot_general(
        left_side, right_side, (((1,), (1,)), ((), ())), preferred_element_type=jnp.float32
    )


def over_rows(left_side, right_side):
    return lax.dot_general(
        left_side, right_side, (((0,), (0,)), ((), ())), preferred_element_type=jnp.float32
    )


def rms_scale(values):
    return lax.rsqrt(jnp.mean(values * values, -1, keepdims=True) + epsilon)


def params(count):
    return pltpu.CompilerParams(
        dimension_semantics=("arbitrary",) * count, vmem_limit_bytes=60 * 1024 * 1024
    )


def whole(shape, single=True):
    zeros = (0,) * len(shape)
    if single:
        return pl.BlockSpec(shape, lambda *ids: zeros, pipeline_mode=pl.Buffered(1))
    return pl.BlockSpec(shape, lambda *ids: zeros)


def rope_tables(token_positions):
    frequency = rope_base ** (-jnp.arange(HEAD_DIM // 2, dtype=jnp.float32) * 2.0 / HEAD_DIM)
    angles = token_positions.astype(jnp.float32)[..., None] * frequency
    cosine, sine_part = jnp.cos(angles), jnp.sin(angles)
    return (
        jnp.concatenate([cosine, cosine], -1),
        jnp.concatenate([-sine_part, sine_part], -1),
    )


def swapped_halves(values):
    width = values.shape[1]
    lane = lax.broadcasted_iota(jnp.int32, values.shape, 1)
    ahead = pltpu.roll(values, width - HEAD_DIM // 2, 1)
    behind = pltpu.roll(values, HEAD_DIM // 2, 1)
    return jnp.where(lane % HEAD_DIM < HEAD_DIM // 2, ahead, behind)


def project_in(rows_in, gain_row, fused_weight, cosine, sine_part):
    tokens, width = rows_in.shape
    step_width = 2 * FUSED_GROUP

    def kernel(rows, gain, weight, cos_ref, sin_ref, fused, normed):
        @pl.when(pl.program_id(0) == 0)
        def _():
            values = rows[...].astype(jnp.float32)
            normed[...] = (values * rms_scale(values) * gain[...]).astype(jnp.bfloat16)

        product = plain(normed[...], weight[...])
        rotated = (product * cos_ref[...] + swapped_halves(product) * sin_ref[...]).astype(
            jnp.bfloat16
        )
        fused[0] = rotated[:, :FUSED_GROUP]
        fused[1] = rotated[:, FUSED_GROUP:]

    return pl.pallas_call(
        kernel,
        grid=(KEY_VALUE_HEADS // 2,),
        in_specs=[
            whole((tokens, width)),
            whole((1, width)),
            pl.BlockSpec((width, step_width), lambda i: (0, i)),
            whole((tokens, step_width)),
            whole((tokens, step_width)),
        ],
        out_specs=[
            pl.BlockSpec((2, tokens, FUSED_GROUP), lambda i: (i, 0, 0)),
            whole((tokens, width)),
        ],
        out_shape=[
            jax.ShapeDtypeStruct((KEY_VALUE_HEADS, tokens, FUSED_GROUP), jnp.bfloat16),
            jax.ShapeDtypeStruct((tokens, width), jnp.bfloat16),
        ],
        name="project_in",
        compiler_params=params(1),
    )(rows_in, gain_row, fused_weight, cosine, sine_part)


def head_probs(query_head, key_rows, visible):
    scores = jnp.where(visible, turned(query_head, key_rows) * HEAD_DIM ** (-0.5), mask_value)
    weights = jnp.exp(scores - jnp.max(scores, -1, keepdims=True))
    return weights * (1.0 / jnp.sum(weights, -1, keepdims=True))


def attend(fused_rows, row_positions, column_positions, lengths_here):
    n_ctx, sequences, span, unused = fused_rows.shape
    seq_len = n_ctx * span
    blocks = max(1, min(n_ctx, 512 * 512 // seq_len // span))
    tile = blocks * span

    def kernel(lengths_ref, query_ref, key_ref, row_ref, column_ref, out_ref):
        length = lengths_ref[pl.program_id(0)]
        fused_keys = key_ref[...].reshape(seq_len, FUSED_GROUP)
        key_rows = fused_keys[:, QUERY_GROUP : QUERY_GROUP + HEAD_DIM]
        value_rows = fused_keys[:, QUERY_GROUP + HEAD_DIM :]
        queries = query_ref[...].reshape(tile, FUSED_GROUP)
        key_pos = column_ref[:1, :]
        visible = (key_pos <= row_ref[:, :1]) & (key_pos < length)
        outs = []
        for head in range(GROUP):
            prob = head_probs(queries[:, head * HEAD_DIM : (head + 1) * HEAD_DIM], key_rows, visible)
            outs.append(plain(prob.astype(jnp.bfloat16), value_rows).astype(jnp.bfloat16))
        out_ref[...] = jnp.concatenate(outs, 1).reshape(blocks, 1, span, QUERY_GROUP)

    return pl.pallas_call(
        kernel,
        grid_spec=pltpu.PrefetchScalarGridSpec(
            num_scalar_prefetch=1,
            grid=(sequences, n_ctx // blocks),
            in_specs=[
                pl.BlockSpec((blocks, 1, span, FUSED_GROUP), lambda s, i, n: (i, s, 0, 0)),
                pl.BlockSpec((n_ctx, 1, span, FUSED_GROUP), lambda s, i, n: (0, s, 0, 0)),
                pl.BlockSpec((tile, LANES), lambda s, i, n: (i, 0)),
                pl.BlockSpec((8, seq_len), lambda s, i, n: (0, 0)),
            ],
            out_specs=pl.BlockSpec((blocks, 1, span, QUERY_GROUP), lambda s, i, n: (i, s, 0, 0)),
        ),
        out_shape=jax.ShapeDtypeStruct((n_ctx, sequences, span, QUERY_GROUP), jnp.bfloat16),
        name="attend",
        compiler_params=params(2),
    )(lengths_here, fused_rows, fused_rows, row_positions, column_positions)


def attend_back(
    fused_rows, d_attended, row_positions, column_positions, cosine, sine_part, lengths_here
):
    n_ctx, sequences, span, unused = fused_rows.shape
    seq_len = n_ctx * span
    blocks = max(1, min(n_ctx, 512 * 512 // seq_len // span))
    tile = blocks * span
    padded = FUSED_GROUP + HEAD_DIM

    def kernel(
        lengths_ref,
        query_ref,
        key_ref,
        d_ref,
        row_ref,
        column_ref,
        cos_ref,
        sin_ref,
        out_ref,
        d_query_keep,
        d_key_keep,
        d_value_keep,
    ):
        part = pl.program_id(1)
        length = lengths_ref[pl.program_id(0)]
        fused_keys = key_ref[...].reshape(seq_len, FUSED_GROUP)
        key_rows = fused_keys[:, QUERY_GROUP : QUERY_GROUP + HEAD_DIM]
        value_rows = fused_keys[:, QUERY_GROUP + HEAD_DIM :]
        queries = query_ref[...].reshape(tile, FUSED_GROUP)
        d_rows = d_ref[...].reshape(tile, QUERY_GROUP)
        key_pos = column_ref[:1, :]
        visible = (key_pos <= row_ref[:, :1]) & (key_pos < length)

        @pl.when(part == 0)
        def _():
            d_key_keep[...] = jnp.zeros_like(d_key_keep)
            d_value_keep[...] = jnp.zeros_like(d_value_keep)

        d_queries = []
        for head in range(GROUP):
            lanes = slice(head * HEAD_DIM, (head + 1) * HEAD_DIM)
            query_head, d_head = queries[:, lanes], d_rows[:, lanes]
            prob = head_probs(query_head, key_rows, visible)
            d_prob = turned(d_head, value_rows)
            delta = jnp.sum(prob * d_prob, -1, keepdims=True)
            d_score = (prob * (d_prob - delta) * HEAD_DIM ** (-0.5)).astype(jnp.bfloat16)
            d_queries.append(plain(d_score, key_rows))
            d_key_keep[...] += over_rows(d_score, query_head)
            d_value_keep[...] += over_rows(prob.astype(jnp.bfloat16), d_head)
        d_query_keep[pl.ds(pl.multiple_of(part * tile, tile), tile), :] = jnp.concatenate(
            d_queries, 1
        )

        @pl.when(part == pl.num_programs(1) - 1)
        def _():
            turned_part = jnp.concatenate([d_query_keep[...], d_key_keep[...]], 1)
            table_cos = jnp.concatenate([cos_ref[...], cos_ref[...]], 1)
            table_sin = jnp.concatenate([sin_ref[...], sin_ref[...]], 1)
            back = turned_part * table_cos - swapped_halves(turned_part) * table_sin
            out_ref[...] = (
                jnp.concatenate([back, d_value_keep[...]], 1)
                .astype(jnp.bfloat16)
                .reshape(n_ctx, 1, span, FUSED_GROUP)
            )

    return pl.pallas_call(
        kernel,
        grid_spec=pltpu.PrefetchScalarGridSpec(
            num_scalar_prefetch=1,
            grid=(sequences, n_ctx // blocks),
            in_specs=[
                pl.BlockSpec((blocks, 1, span, FUSED_GROUP), lambda s, i, n: (i, s, 0, 0)),
                pl.BlockSpec((n_ctx, 1, span, FUSED_GROUP), lambda s, i, n: (0, s, 0, 0)),
                pl.BlockSpec((blocks, 1, span, QUERY_GROUP), lambda s, i, n: (i, s, 0, 0)),
                pl.BlockSpec((tile, LANES), lambda s, i, n: (i, 0)),
                pl.BlockSpec((8, seq_len), lambda s, i, n: (0, 0)),
                pl.BlockSpec((seq_len, LANES), lambda s, i, n: (0, 0)),
                pl.BlockSpec((seq_len, LANES), lambda s, i, n: (0, 0)),
            ],
            out_specs=pl.BlockSpec((n_ctx, 1, span, FUSED_GROUP), lambda s, i, n: (0, s, 0, 0)),
            scratch_shapes=[
                pltpu.VMEM((seq_len, QUERY_GROUP), jnp.float32),
                pltpu.VMEM((seq_len, HEAD_DIM), jnp.float32),
                pltpu.VMEM((seq_len, HEAD_DIM), jnp.float32),
            ],
        ),
        out_shape=jax.ShapeDtypeStruct((n_ctx, sequences, span, FUSED_GROUP), jnp.bfloat16),
        name="attend_back",
        compiler_params=params(2),
    )(
        lengths_here,
        fused_rows,
        fused_rows,
        d_attended,
        row_positions,
        column_positions,
        cosine,
        sine_part,
    )


def project_out(attended_groups, rows_in, out_weight, gain_row):
    tokens, width = rows_in.shape

    def kernel(groups, rows, weight, gain, residual, normed, joined):
        attended = jnp.concatenate([groups[j] for j in range(KEY_VALUE_HEADS)], 1)
        joined[...] = attended
        total = rows[...].astype(jnp.float32) + plain(attended, weight[...])
        residual[...] = total
        normed[...] = (total * rms_scale(total) * gain[...]).astype(jnp.bfloat16)

    return pl.pallas_call(
        kernel,
        grid=(1,),
        in_specs=[
            whole(attended_groups.shape),
            whole((tokens, width)),
            whole((QUERY_HEADS * HEAD_DIM, width)),
            whole((1, width)),
        ],
        out_specs=[
            whole((tokens, width)),
            whole((tokens, width)),
            whole((tokens, QUERY_HEADS * HEAD_DIM)),
        ],
        out_shape=[
            jax.ShapeDtypeStruct((tokens, width), jnp.float32),
            jax.ShapeDtypeStruct((tokens, width), jnp.bfloat16),
            jax.ShapeDtypeStruct((tokens, QUERY_HEADS * HEAD_DIM), jnp.bfloat16),
        ],
        name="project_out",
        compiler_params=params(1),
    )(attended_groups, rows_in, out_weight, gain_row)


def expert_chunk(
    first_expert,
    expert_total,
    side,
    ctx_parts,
    normed_rows,
    normed_turned,
    cotangent_rows,
    cotangent_turned,
    gate_table,
    w_gate,
    w_up,
    w_down,
    kept,
):
    rows, width = normed_rows.shape
    experts, unused, hidden = w_gate.shape
    pair_width = 2 * hidden
    slab = width // (2 * ctx_parts)
    row_block = min(ROW_BLOCK, rows)

    def kernel(
        side_ref,
        normed,
        normed_t,
        cotan,
        cotan_t,
        gates,
        gate_w,
        up_w,
        down_w,
        *rest,
    ):
        stay, leave, acts, d_gates = rest[-4:]
        first = first_expert + 2 * pl.program_id(0)

        @pl.when(pl.program_id(0) == 0)
        def _():
            d_gates[...] = jnp.zeros_like(d_gates)

        def joined(pair_ref):
            return jnp.concatenate([pair_ref[0], pair_ref[1]], axis=1)

        gate_pair, up_pair, down_pair = joined(gate_w), joined(up_w), joined(down_w)
        lane = lax.broadcasted_iota(jnp.int32, (row_block, LANES), 1)

        def row_step(block, carry):
            span = pl.ds(pl.multiple_of(block * row_block, row_block), row_block)
            normed_part, cotan_part = normed[span, :], cotan[span, :]
            gate_part = gates[span, :]
            slot_gate = jnp.concatenate(
                [
                    jnp.broadcast_to(
                        jnp.sum(
                            jnp.where(lane == first + j, gate_part, 0.0), axis=1, keepdims=True
                        ),
                        (row_block, hidden),
                    )
                    for j in range(2)
                ],
                axis=1,
            )
            gate_pre = plain(normed_part, gate_pair)
            up_pre = plain(normed_part, up_pair)
            d_scaled = plain(cotan_part, down_pair)
            sigmoid_gate = jax.nn.sigmoid(gate_pre)
            silu_gate = gate_pre * sigmoid_gate
            scaled = (slot_gate * silu_gate * up_pre).astype(jnp.bfloat16)
            gate_term = d_scaled * silu_gate * up_pre
            d_gate_part = d_gates[span, :]
            for j in range(2):
                d_gate_part = d_gate_part + jnp.where(
                    lane == first + j,
                    jnp.sum(gate_term[:, j * hidden : (j + 1) * hidden], axis=1, keepdims=True),
                    0.0,
                )
            d_gates[span, :] = d_gate_part
            d_act = d_scaled * slot_gate
            acts[0, 0, span, :] = scaled
            acts[1, 0, span, :] = (
                d_act * up_pre * (sigmoid_gate + silu_gate * (1.0 - sigmoid_gate))
            ).astype(jnp.bfloat16)
            acts[2, 0, span, :] = (d_act * silu_gate).astype(jnp.bfloat16)
            return carry

        lax.fori_loop(0, rows // row_block, row_step, 0)
        for target, choice in ((leave, 1 - side_ref[0]), (stay, side_ref[0])):
            for kind, source in ((0, normed_t), (1, normed_t), (2, cotan_t)):
                left_side = jnp.concatenate(
                    [
                        source[pl.ds(pl.multiple_of((2 * part + choice) * slab, 16), slab), :]
                        for part in range(ctx_parts)
                    ],
                    0,
                )
                term = plain(left_side, acts[(1, 2, 0)[kind], 0]).astype(jnp.bfloat16)
                for j in range(2):
                    target[kind, j] = term[:, j * hidden : (j + 1) * hidden]

    start = first_expert // 2

    def weight_block():
        return pl.BlockSpec((2, width, hidden), lambda pair, side: (pair + start, 0, 0))

    half_block = pl.BlockSpec((3, 2, width // 2, hidden), lambda pair, side: (0, pair, 0, 0))
    half_shape = jax.ShapeDtypeStruct((3, expert_total, width // 2, hidden), jnp.bfloat16)
    extra = [] if kept is None else [kept]
    return pl.pallas_call(
        kernel,
        grid_spec=pltpu.PrefetchScalarGridSpec(
            num_scalar_prefetch=1,
            grid=(expert_total // 2,),
            in_specs=[
                whole((rows, width)),
                whole((width, rows)),
                whole((rows, width)),
                whole((width, rows)),
                whole((rows, LANES)),
                weight_block(),
                weight_block(),
                weight_block(),
            ]
            + [pl.BlockSpec(memory_space=pl.ANY)] * len(extra),
            out_specs=[
                half_block,
                half_block,
                pl.BlockSpec(
                    (3, 1, rows, pair_width), lambda pair, side: (0, pair + start, 0, 0)
                ),
                whole((rows, LANES)),
            ],
        ),
        out_shape=[
            half_shape,
            half_shape,
            jax.ShapeDtypeStruct((3, experts // 2, rows, pair_width), jnp.bfloat16),
            jax.ShapeDtypeStruct((rows, LANES), jnp.float32),
        ],
        input_output_aliases={9: 2} if extra else {},
        name="expert_chunk",
        compiler_params=params(1),
    )(
        side,
        normed_rows,
        normed_turned,
        cotangent_rows,
        cotangent_turned,
        gate_table,
        w_gate,
        w_up,
        w_down,
        *extra,
    )


def expert_rows(kinds, weights, acts, d_gates, route_hot):
    unused, pairs, rows, pair_width = acts.shape
    experts, width, hidden = weights[0].shape
    step_pairs = 4
    total = len(kinds)
    gate_lanes = 0 if d_gates is None else LANES
    row_block = min(256, rows)

    def kernel(*refs):
        act_refs, weight_refs = refs[:total], refs[total : 2 * total]
        keep = refs[-1]
        out_ref = refs[-2]
        step = pl.program_id(0)
        right_side = jnp.concatenate(
            [ref[j] for ref in weight_refs for j in range(2 * step_pairs)], 1
        )

        def row_step(block, carry):
            span = pl.ds(pl.multiple_of(block * row_block, row_block), row_block)
            left_side = jnp.concatenate(
                [ref[0, j, span, :] for ref in act_refs for j in range(step_pairs)], 1
            )
            term = turned(left_side, right_side)

            @pl.when(step == 0)
            def _():
                keep[span, :] = term

            @pl.when((step > 0) & (step < pl.num_programs(0) - 1))
            def _():
                keep[span, :] += term

            @pl.when(step == pl.num_programs(0) - 1)
            def _():
                out_ref[span, :width] = (keep[span, :] + term).astype(jnp.bfloat16)
                if gate_lanes:
                    out_ref[span, width:] = (
                        refs[2 * total][span, :] * refs[2 * total + 1][span, :]
                    ).astype(jnp.bfloat16)

            return carry

        lax.fori_loop(0, rows // row_block, row_step, 0)

    def act_block(kind):
        return pl.BlockSpec((1, step_pairs, rows, pair_width), lambda i: (kind, i, 0, 0))

    extra = [] if d_gates is None else [d_gates, route_hot]
    return pl.pallas_call(
        kernel,
        grid=(pairs // step_pairs,),
        in_specs=[act_block(kind) for kind in kinds]
        + [pl.BlockSpec((2 * step_pairs, width, hidden), lambda i: (i, 0, 0))] * total
        + [whole((rows, LANES))] * len(extra),
        out_specs=whole((rows, width + gate_lanes)),
        out_shape=jax.ShapeDtypeStruct((rows, width + gate_lanes), jnp.bfloat16),
        scratch_shapes=[pltpu.VMEM((rows, width), jnp.float32)],
        name="expert_rows",
        compiler_params=params(1),
    )(*([acts] * total), *weights, *extra)


def middle_back(d_packed, probs, share_row, live_lanes, residual, cotangent_rows, gain_row, weight):
    tokens, width = residual.shape

    def kernel(
        packed,
        prob_ref,
        share_ref,
        live_ref,
        residual_ref,
        cotan_ref,
        gain_ref,
        weight_ref,
        d_residual,
        d_branch,
        d_logits,
        d_gain,
        d_groups,
    ):
        prob = prob_ref[...]
        live = live_ref[...]
        d_prob = packed[:, width:].astype(jnp.float32) + share_ref[...] * live
        logits = (prob * (d_prob - jnp.sum(prob * d_prob, -1, keepdims=True))).astype(jnp.bfloat16)
        d_logits[...] = logits
        d_normed = packed[:, :width].astype(jnp.float32) + turned(logits, weight_ref[:, width:])
        total = residual_ref[...]
        scale = rms_scale(total)
        unit = total * scale
        d_gain[...] = jnp.broadcast_to(jnp.sum(d_normed * unit, 0, keepdims=True), (8, width))
        d_unit = d_normed * gain_ref[...]
        d_total = cotan_ref[...].astype(jnp.float32) * live[:, :1] + scale * (
            d_unit - unit * jnp.mean(d_unit * unit, -1, keepdims=True)
        )
        d_residual[...] = d_total
        low = d_total.astype(jnp.bfloat16)
        d_branch[...] = low
        for j in range(KEY_VALUE_HEADS):
            d_groups[j] = turned(
                low, weight_ref[j * QUERY_GROUP : (j + 1) * QUERY_GROUP, :width]
            ).astype(jnp.bfloat16)

    inputs = (d_packed, probs, share_row, live_lanes, residual, cotangent_rows, gain_row, weight)
    out_shape = [
        jax.ShapeDtypeStruct((tokens, width), jnp.float32),
        jax.ShapeDtypeStruct((tokens, width), jnp.bfloat16),
        jax.ShapeDtypeStruct((tokens, LANES), jnp.bfloat16),
        jax.ShapeDtypeStruct((8, width), jnp.float32),
        jax.ShapeDtypeStruct((KEY_VALUE_HEADS, tokens, QUERY_GROUP), jnp.bfloat16),
    ]
    return pl.pallas_call(
        kernel,
        grid=(1,),
        in_specs=[whole(value.shape) for value in inputs],
        out_specs=[whole(value.shape) for value in out_shape],
        out_shape=out_shape,
        name="middle_back",
        compiler_params=params(1),
    )(*inputs)


def early_grads(attended, d_branch, normed, d_logits, d_gain, gain_lane):
    tokens, width = normed.shape
    block = width // 3

    def kernel(attended_ref, branch_ref, normed_ref, logits_ref, gain_ref, out_ref):
        out_ref[:, :width] = over_rows(attended_ref[...], branch_ref[...]).astype(jnp.bfloat16)
        side_term = over_rows(normed_ref[...], logits_ref[...])
        column = jnp.broadcast_to(gain_ref[:1, :], (LANES, block)).T
        lane = lax.broadcasted_iota(jnp.int32, (block, LANES), 1)
        out_ref[:, width:] = jnp.where(lane == gain_lane, column, side_term).astype(jnp.bfloat16)

    return pl.pallas_call(
        kernel,
        grid=(3,),
        in_specs=[
            pl.BlockSpec((tokens, block), lambda i: (0, i)),
            whole((tokens, width)),
            pl.BlockSpec((tokens, block), lambda i: (0, i)),
            whole((tokens, LANES)),
            pl.BlockSpec((8, block), lambda i: (0, i)),
        ],
        out_specs=pl.BlockSpec((block, width + LANES), lambda i: (i, 0)),
        out_shape=jax.ShapeDtypeStruct((width, width + LANES), jnp.bfloat16),
        name="early_grads",
        compiler_params=params(1),
    )(attended, d_branch, normed, d_logits, d_gain)


def project_back(d_fused, fused_weight, normed, rows_in, gain_row, d_residual):
    tokens, width = rows_in.shape
    step_width = 2 * FUSED_GROUP
    steps = KEY_VALUE_HEADS // 2

    def kernel(d_ref, weight, normed_ref, rows, gain, d_residual_ref, late, d_input, keep):
        step = pl.program_id(0)
        d_pair = jnp.concatenate([d_ref[0], d_ref[1]], 1)
        late[:, pl.ds(pl.multiple_of(step * step_width, LANES), step_width)] = over_rows(
            normed_ref[...], d_pair
        ).astype(jnp.bfloat16)
        term = turned(d_pair, weight[...])

        @pl.when(step == 0)
        def _():
            keep[...] = term

        @pl.when(step > 0)
        def _():
            keep[...] += term

        @pl.when(step == steps - 1)
        def _():
            values = rows[...].astype(jnp.float32)
            scale = rms_scale(values)
            unit = values * scale
            d_normed = keep[...]
            d_unit = d_normed * gain[...]
            d_input[...] = d_residual_ref[...] + scale * (
                d_unit - unit * jnp.mean(d_unit * unit, -1, keepdims=True)
            )
            d_gain = jnp.sum(d_normed * unit, 0, keepdims=True)
            late[:, FUSED_WIDTH:] = jnp.broadcast_to(d_gain, (LANES, width)).T.astype(jnp.bfloat16)

    return pl.pallas_call(
        kernel,
        grid=(steps,),
        in_specs=[
            pl.BlockSpec((2, tokens, FUSED_GROUP), lambda i: (i, 0, 0)),
            pl.BlockSpec((width, step_width), lambda i: (0, i)),
            whole((tokens, width)),
            whole((tokens, width)),
            whole((1, width)),
            whole((tokens, width)),
        ],
        out_specs=[whole((width, FUSED_WIDTH + LANES)), whole((tokens, width))],
        out_shape=[
            jax.ShapeDtypeStruct((width, FUSED_WIDTH + LANES), jnp.bfloat16),
            jax.ShapeDtypeStruct((tokens, width), jnp.float32),
        ],
        scratch_shapes=[pltpu.VMEM((tokens, width), jnp.float32)],
        name="project_back",
        compiler_params=params(1),
    )(d_fused, fused_weight, normed, rows_in, gain_row, d_residual)


def local(
    layer_input,
    gain_attn,
    w_query,
    key_projection_weight,
    value_projection_weight,
    w_out,
    gain_ffn,
    w_router,
    w_gate,
    w_up,
    w_down,
    routes,
    lengths,
    cotangent,
):
    ctx_parts = lax.axis_size("z")
    n_ctx = 2 * ctx_parts
    n_shard = 2 * lax.axis_size("x")
    ctx_side = lax.axis_index("y")
    ctx_pos = 2 * lax.axis_index("z") + ctx_side
    shard_pos = 2 * lax.axis_index("x") + lax.axis_index("k")
    local_sequences = layer_input.shape[0]
    half_rows = layer_input.shape[3]
    model_width = layer_input.shape[4]
    sequence_rows = 2 * half_rows
    tokens = local_sequences * sequence_rows
    seq_len = n_ctx * sequence_rows
    experts = w_gate.shape[0]
    top_k = routes.shape[4]
    gathered_rows = n_shard * tokens
    head_shares = n_ctx // KEY_VALUE_HEADS
    here_sequences = local_sequences // head_shares
    width_rows = gain_attn.shape[0]

    def fused_columns(query_part, key_part, value_part):
        rows = query_part.shape[0]
        return jnp.concatenate(
            [
                query_part.reshape(rows, KEY_VALUE_HEADS, QUERY_GROUP),
                key_part.reshape(rows, KEY_VALUE_HEADS, HEAD_DIM),
                value_part.reshape(rows, KEY_VALUE_HEADS, HEAD_DIM),
            ],
            -1,
        ).reshape(rows, FUSED_WIDTH)

    fused_weight = lax.all_gather(
        jnp.concatenate(
            [
                fused_columns(w_query, key_projection_weight, value_projection_weight),
                jnp.pad(gain_attn[:, None], ((0, 0), (0, LANES - 1))),
            ],
            1,
        ),
        SHARD,
        axis=0,
        tiled=True,
    )
    out_weight = lax.all_gather(
        jnp.concatenate(
            [
                w_out,
                w_router,
                gain_ffn[:, None],
                jnp.zeros((width_rows, LANES - experts - 1), jnp.bfloat16),
            ],
            1,
        ),
        SHARD,
        axis=0,
        tiled=True,
    )
    gain_one = fused_weight[:, FUSED_WIDTH].astype(jnp.float32)[None, :]
    gain_two = out_weight[:, model_width + experts].astype(jnp.float32)[None, :]
    router_matrix = out_weight[:, model_width : model_width + experts]

    slots = jnp.arange(seq_len, dtype=jnp.int32)
    slot_ctx, slot_row = slots // sequence_rows, slots % sequence_rows
    all_positions = (
        jnp.where(slot_row < half_rows, slot_ctx, 2 * n_ctx - 1 - slot_ctx) * half_rows
        + slot_row % half_rows
    )
    local_positions = lax.dynamic_slice_in_dim(all_positions, ctx_pos * sequence_rows, sequence_rows)
    seq_lengths = lax.dynamic_slice_in_dim(lengths, shard_pos * local_sequences, local_sequences)
    lengths_here = lax.dynamic_slice_in_dim(
        seq_lengths, (ctx_pos % head_shares) * here_sequences, here_sequences
    )
    live_rows = (local_positions[None, :] < seq_lengths[:, None]).reshape(tokens)
    live_lanes = jnp.broadcast_to(live_rows.astype(jnp.float32)[:, None], (tokens, LANES))
    live_group = (
        (local_positions[None, :] < lengths[:, None]).astype(jnp.float32).reshape(gathered_rows)
    )
    row_positions = jnp.broadcast_to(all_positions[:, None], (seq_len, LANES))
    column_positions = jnp.broadcast_to(all_positions[None, :], (8, seq_len))
    every_cos, every_sin = rope_tables(all_positions)
    own_cos, own_sin = rope_tables(local_positions)
    still = jnp.ones_like(own_cos)
    step_cos = jnp.tile(
        jnp.concatenate([own_cos] * (GROUP + 1) + [still], 1), (local_sequences, 2)
    )
    step_sin = jnp.tile(
        jnp.concatenate([own_sin] * (GROUP + 1) + [0.0 * still], 1), (local_sequences, 2)
    )
    pair_cos, pair_sin = jnp.tile(every_cos, (1, 2)), jnp.tile(every_sin, (1, 2))

    rows_in = layer_input.reshape(tokens, model_width)
    cotangent_rows = cotangent.reshape(tokens, model_width)
    d_moe = jnp.where(live_rows[:, None], cotangent_rows, jnp.bfloat16(0.0))
    d_moe_all = lax.all_gather(d_moe, SHARD, axis=0, tiled=True)
    d_moe_turned = d_moe_all.T

    def exchange(groups):
        return lax.all_to_all(groups, CTX, 0, 0, tiled=True)

    fused_own, first_normed = project_in(rows_in, gain_one, fused_weight, step_cos, step_sin)
    fused_rows = exchange(
        fused_own.reshape(n_ctx, here_sequences, sequence_rows, FUSED_GROUP)
    )
    attended_rows = attend(fused_rows, row_positions, column_positions, lengths_here)
    attended_groups = exchange(attended_rows).reshape(KEY_VALUE_HEADS, tokens, QUERY_GROUP)
    residual, second_normed, attended_low = project_out(
        attended_groups, rows_in, out_weight, gain_two
    )

    normed_all = lax.all_gather(second_normed, SHARD, axis=0, tiled=True)
    normed_turned = normed_all.T
    router_probs = jax.nn.softmax(plain(normed_all, router_matrix), axis=-1)
    route_hot = jnp.any(
        routes.reshape(gathered_rows, top_k, 1) == jnp.arange(experts, dtype=jnp.int32), axis=1
    ).astype(jnp.float32)
    lane_pad = ((0, 0), (0, LANES - experts))
    prob_table = jnp.pad(router_probs, lane_pad)
    hot_table = jnp.pad(route_hot, lane_pad)
    gate_table = prob_table * hot_table

    side = ctx_side.astype(jnp.int32).reshape(1)
    swap = [(0, 1), (1, 0)]
    acts, d_gates, reduced = None, None, []
    first_expert = 0
    for chunk in CHUNKS:
        stay, leave, acts, gate_piece = expert_chunk(
            first_expert,
            chunk,
            side,
            ctx_parts,
            normed_all,
            normed_turned,
            d_moe_all,
            d_moe_turned,
            gate_table,
            w_gate,
            w_up,
            w_down,
            acts,
        )
        first_expert += chunk
        d_gates = gate_piece if d_gates is None else d_gates + gate_piece
        arrived = lax.ppermute(leave, "y", swap)
        halved = (stay.astype(jnp.float32) + arrived.astype(jnp.float32)).astype(jnp.bfloat16)
        reduced.append(lax.psum_scatter(halved, "z", scatter_dimension=2, tiled=True))

    d_packed = expert_rows((1, 2), (w_gate, w_up), acts, d_gates, hot_table)
    d_packed_own = lax.psum_scatter(d_packed, SHARD, scatter_dimension=0, tiled=True)
    moe_rows = expert_rows((0,), (w_down,), acts, None, None)
    moe_own = lax.psum_scatter(moe_rows, SHARD, scatter_dimension=0, tiled=True)
    layer_output = (
        (residual + moe_own.astype(jnp.float32)).astype(jnp.bfloat16).reshape(layer_input.shape)
    )

    group_sums = jnp.stack(
        [jnp.sum(route_hot * live_group[:, None], 0), jnp.sum(router_probs * live_group[:, None], 0)]
    )
    all_sums = lax.psum(group_sums, CTX)
    live_all = jnp.sum(lengths).astype(jnp.float32)
    route_share = all_sums[0] / (top_k * live_all)
    aux_loss = experts * jnp.sum(route_share * all_sums[1] / live_all)
    share_row = jnp.pad((loss_weight * experts / live_all) * route_share[None, :], lane_pad)

    own_probs = lax.dynamic_slice_in_dim(prob_table, shard_pos * tokens, tokens, 0)
    d_residual, d_branch, d_logits, d_gain_two, d_groups = middle_back(
        d_packed_own,
        own_probs,
        share_row,
        live_lanes,
        residual,
        cotangent_rows,
        gain_two,
        out_weight,
    )
    d_attended = exchange(d_groups.reshape(n_ctx, here_sequences, sequence_rows, QUERY_GROUP))
    early_terms = early_grads(attended_low, d_branch, second_normed, d_logits, d_gain_two, experts)
    d_fused_rows = attend_back(
        fused_rows,
        d_attended,
        row_positions,
        column_positions,
        pair_cos,
        pair_sin,
        lengths_here,
    )
    d_fused = exchange(d_fused_rows).reshape(KEY_VALUE_HEADS, tokens, FUSED_GROUP)
    late_terms, grad_input = project_back(
        d_fused, fused_weight, first_normed, rows_in, gain_one, d_residual
    )
    early_rows = lax.psum_scatter(early_terms, EVERY, scatter_dimension=0, tiled=True)
    late_rows = lax.psum_scatter(late_terms, EVERY, scatter_dimension=0, tiled=True)
    early_rows, late_rows = early_rows.astype(jnp.float32), late_rows.astype(jnp.float32)
    late_groups = late_rows[:, :FUSED_WIDTH].reshape(-1, KEY_VALUE_HEADS, FUSED_GROUP)
    own_rows = late_rows.shape[0]
    grads = [
        jnp.concatenate([piece[kind] for piece in reduced], 0).astype(jnp.float32)
        for kind in range(3)
    ]
    return (
        layer_output,
        grad_input.reshape(layer_input.shape),
        late_rows[:, FUSED_WIDTH],
        late_groups[:, :, :QUERY_GROUP].reshape(own_rows, -1),
        late_groups[:, :, QUERY_GROUP : QUERY_GROUP + HEAD_DIM].reshape(own_rows, -1),
        late_groups[:, :, QUERY_GROUP + HEAD_DIM :].reshape(own_rows, -1),
        early_rows[:, :model_width],
        early_rows[:, model_width + experts],
        early_rows[:, model_width : model_width + experts],
        grads[0],
        grads[1],
        grads[2],
        aux_loss,
    )


def solution(mesh):
    n_ctx, n_shard = mesh.shape["ctx"], mesh.shape["fsdp"]
    fine = Mesh(mesh.devices.reshape(n_ctx // 2, 2, n_shard // 2, 2), EVERY)
    placed = (
        P(SHARD, CTX, None, None, None),
        P(SHARD),
        P(SHARD, None),
        P(SHARD, None),
        P(SHARD, None),
        P(SHARD, None),
        P(SHARD),
        P(SHARD, None),
        P(None, None, SHARD),
        P(None, None, SHARD),
        P(None, None, SHARD),
        P(None, CTX, None, None, None),
        P(),
        P(SHARD, CTX, None, None, None),
    )
    return jax.shard_map(
        local,
        mesh=fine,
        in_specs=placed,
        out_specs=(
            P(SHARD, CTX, None, None, None),
            P(SHARD, CTX, None, None, None),
            P(EVERY),
            P(EVERY, None),
            P(EVERY, None),
            P(EVERY, None),
            P(EVERY, None),
            P(EVERY),
            P(EVERY, None),
            P(None, CTX, SHARD),
            P(None, CTX, SHARD),
            P(None, CTX, SHARD),
            P(),
        ),
        check_vma=False,
    )
```

```python
import jax
import jax.numpy as jnp
from jax import lax
from jax.experimental import pallas as pl
from jax.experimental.pallas import tpu as pltpu
from jax.sharding import Mesh
from jax.sharding import PartitionSpec as P


QUERY_HEADS = 24
KEY_VALUE_HEADS = 8
HEAD_DIM = 64
GROUP = QUERY_HEADS // KEY_VALUE_HEADS
QUERY_GROUP = GROUP * HEAD_DIM
FUSED_GROUP = QUERY_GROUP + 2 * HEAD_DIM
FUSED_WIDTH = KEY_VALUE_HEADS * FUSED_GROUP
LANES = 128
ROW_BLOCK = 512
CHUNKS = (8, 8, 8, 8, 8)
CTX = ("z", "y")
SHARD = ("x", "k")
EVERY = ("z", "y", "x", "k")

epsilon = 1e-05
rope_base = 10000.0
loss_weight = 0.01
mask_value = -1e30


def plain(left_side, right_side):
    return jnp.dot(left_side, right_side, preferred_element_type=jnp.float32)


def turned(left_side, right_side):
    return lax.dot_general(
        left_side, right_side, (((1,), (1,)), ((), ())), preferred_element_type=jnp.float32
    )


def over_rows(left_side, right_side):
    return lax.dot_general(
        left_side, right_side, (((0,), (0,)), ((), ())), preferred_element_type=jnp.float32
    )


def rms_scale(values):
    return lax.rsqrt(jnp.mean(values * values, -1, keepdims=True) + epsilon)


def params(count):
    return pltpu.CompilerParams(
        dimension_semantics=("arbitrary",) * count, vmem_limit_bytes=60 * 1024 * 1024
    )


def whole(shape, single=True):
    zeros = (0,) * len(shape)
    if single:
        return pl.BlockSpec(shape, lambda *ids: zeros, pipeline_mode=pl.Buffered(1))
    return pl.BlockSpec(shape, lambda *ids: zeros)


def rope_tables(token_positions):
    frequency = rope_base ** (-jnp.arange(HEAD_DIM // 2, dtype=jnp.float32) * 2.0 / HEAD_DIM)
    angles = token_positions.astype(jnp.float32)[..., None] * frequency
    cosine, sine_part = jnp.cos(angles), jnp.sin(angles)
    return (
        jnp.concatenate([cosine, cosine], -1),
        jnp.concatenate([-sine_part, sine_part], -1),
    )


def swapped_halves(values):
    width = values.shape[1]
    lane = lax.broadcasted_iota(jnp.int32, values.shape, 1)
    ahead = pltpu.roll(values, width - HEAD_DIM // 2, 1)
    behind = pltpu.roll(values, HEAD_DIM // 2, 1)
    return jnp.where(lane % HEAD_DIM < HEAD_DIM // 2, ahead, behind)


def project_in(rows_in, gain_row, fused_weight, cosine, sine_part):
    tokens, width = rows_in.shape
    query_step, head_step = 2 * QUERY_GROUP, 2 * HEAD_DIM
    rotated_width = query_step + head_step

    def kernel(rows, gain, query_w, key_w, value_w, cos_ref, sin_ref, fused, normed):
        @pl.when(pl.program_id(0) == 0)
        def _():
            values = rows[...].astype(jnp.float32)
            normed[...] = (values * rms_scale(values) * gain[...]).astype(jnp.bfloat16)

        product = plain(
            normed[...], jnp.concatenate([query_w[...], key_w[...], value_w[...]], 1)
        )
        turning = product[:, :rotated_width]
        rotated = (turning * cos_ref[...] + swapped_halves(turning) * sin_ref[...]).astype(
            jnp.bfloat16
        )
        values_low = product[:, rotated_width:].astype(jnp.bfloat16)
        for j in range(2):
            lanes = slice(j * HEAD_DIM, (j + 1) * HEAD_DIM)
            fused[j] = jnp.concatenate(
                [
                    rotated[:, j * QUERY_GROUP : (j + 1) * QUERY_GROUP],
                    rotated[:, query_step:][:, lanes],
                    values_low[:, lanes],
                ],
                1,
            )

    key_start = KEY_VALUE_HEADS * QUERY_GROUP // head_step
    value_start = key_start + KEY_VALUE_HEADS // 2
    return pl.pallas_call(
        kernel,
        grid=(KEY_VALUE_HEADS // 2,),
        in_specs=[
            whole((tokens, width)),
            whole((1, width)),
            pl.BlockSpec((width, query_step), lambda i: (0, i)),
            pl.BlockSpec((width, head_step), lambda i: (0, key_start + i)),
            pl.BlockSpec((width, head_step), lambda i: (0, value_start + i)),
            whole((tokens, rotated_width)),
            whole((tokens, rotated_width)),
        ],
        out_specs=[
            pl.BlockSpec((2, tokens, FUSED_GROUP), lambda i: (i, 0, 0)),
            whole((tokens, width)),
        ],
        out_shape=[
            jax.ShapeDtypeStruct((KEY_VALUE_HEADS, tokens, FUSED_GROUP), jnp.bfloat16),
            jax.ShapeDtypeStruct((tokens, width), jnp.bfloat16),
        ],
        name="project_in",
        compiler_params=params(1),
    )(rows_in, gain_row, fused_weight, fused_weight, fused_weight, cosine, sine_part)


def head_probs(query_head, key_rows, visible):
    scores = jnp.where(visible, turned(query_head, key_rows) * HEAD_DIM ** (-0.5), mask_value)
    weights = jnp.exp(scores - jnp.max(scores, -1, keepdims=True))
    return weights * (1.0 / jnp.sum(weights, -1, keepdims=True))


def attend(fused_rows, row_positions, column_positions, lengths_here):
    n_ctx, sequences, span, _ = fused_rows.shape
    seq_len = n_ctx * span
    blocks = max(1, min(n_ctx, 512 * 512 // seq_len // span))
    tile = blocks * span

    def kernel(lengths_ref, query_ref, key_ref, row_ref, column_ref, out_ref):
        length = lengths_ref[pl.program_id(0)]
        fused_keys = key_ref[...].reshape(seq_len, FUSED_GROUP)
        key_rows = fused_keys[:, QUERY_GROUP : QUERY_GROUP + HEAD_DIM]
        value_rows = fused_keys[:, QUERY_GROUP + HEAD_DIM :]
        queries = query_ref[...].reshape(tile, FUSED_GROUP)
        key_pos = column_ref[:1, :]
        visible = (key_pos <= row_ref[:, :1]) & (key_pos < length)
        outs = []
        for head in range(GROUP):
            prob = head_probs(queries[:, head * HEAD_DIM : (head + 1) * HEAD_DIM], key_rows, visible)
            outs.append(plain(prob.astype(jnp.bfloat16), value_rows).astype(jnp.bfloat16))
        out_ref[...] = jnp.concatenate(outs, 1).reshape(blocks, 1, span, QUERY_GROUP)

    return pl.pallas_call(
        kernel,
        grid_spec=pltpu.PrefetchScalarGridSpec(
            num_scalar_prefetch=1,
            grid=(sequences, n_ctx // blocks),
            in_specs=[
                pl.BlockSpec((blocks, 1, span, FUSED_GROUP), lambda s, i, n: (i, s, 0, 0)),
                pl.BlockSpec((n_ctx, 1, span, FUSED_GROUP), lambda s, i, n: (0, s, 0, 0)),
                pl.BlockSpec((tile, LANES), lambda s, i, n: (i, 0)),
                pl.BlockSpec((8, seq_len), lambda s, i, n: (0, 0)),
            ],
            out_specs=pl.BlockSpec((blocks, 1, span, QUERY_GROUP), lambda s, i, n: (i, s, 0, 0)),
        ),
        out_shape=jax.ShapeDtypeStruct((n_ctx, sequences, span, QUERY_GROUP), jnp.bfloat16),
        name="attend",
        compiler_params=params(2),
    )(lengths_here, fused_rows, fused_rows, row_positions, column_positions)


def attend_back(
    fused_rows, d_attended, row_positions, column_positions, cosine, sine_part, lengths_here
):
    n_ctx, sequences, span, _ = fused_rows.shape
    seq_len = n_ctx * span
    blocks = max(1, min(n_ctx, 512 * 512 // seq_len // span))
    tile = blocks * span

    def kernel(
        lengths_ref,
        query_ref,
        key_ref,
        d_ref,
        row_ref,
        column_ref,
        cos_ref,
        sin_ref,
        out_ref,
        d_query_keep,
        d_key_keep,
        d_value_keep,
    ):
        part = pl.program_id(1)
        length = lengths_ref[pl.program_id(0)]
        fused_keys = key_ref[...].reshape(seq_len, FUSED_GROUP)
        key_rows = fused_keys[:, QUERY_GROUP : QUERY_GROUP + HEAD_DIM]
        value_rows = fused_keys[:, QUERY_GROUP + HEAD_DIM :]
        queries = query_ref[...].reshape(tile, FUSED_GROUP)
        d_rows = d_ref[...].reshape(tile, QUERY_GROUP)
        key_pos = column_ref[:1, :]
        visible = (key_pos <= row_ref[:, :1]) & (key_pos < length)

        @pl.when(part == 0)
        def _():
            d_key_keep[...] = jnp.zeros_like(d_key_keep)
            d_value_keep[...] = jnp.zeros_like(d_value_keep)

        d_queries = []
        for head in range(GROUP):
            lanes = slice(head * HEAD_DIM, (head + 1) * HEAD_DIM)
            query_head, d_head = queries[:, lanes], d_rows[:, lanes]
            prob = head_probs(query_head, key_rows, visible)
            d_prob = turned(d_head, value_rows)
            delta = jnp.sum(prob * d_prob, -1, keepdims=True)
            d_score = (prob * (d_prob - delta) * HEAD_DIM ** (-0.5)).astype(jnp.bfloat16)
            d_queries.append(plain(d_score, key_rows))
            d_key_keep[...] += over_rows(d_score, query_head)
            d_value_keep[...] += over_rows(prob.astype(jnp.bfloat16), d_head)
        d_query_keep[pl.ds(pl.multiple_of(part * tile, tile), tile), :] = jnp.concatenate(
            d_queries, 1
        )

        @pl.when(part == pl.num_programs(1) - 1)
        def _():
            turned_part = jnp.concatenate([d_query_keep[...], d_key_keep[...]], 1)
            table_cos = jnp.concatenate([cos_ref[...], cos_ref[...]], 1)
            table_sin = jnp.concatenate([sin_ref[...], sin_ref[...]], 1)
            back = turned_part * table_cos - swapped_halves(turned_part) * table_sin
            out_ref[...] = (
                jnp.concatenate([back, d_value_keep[...]], 1)
                .astype(jnp.bfloat16)
                .reshape(n_ctx, 1, span, FUSED_GROUP)
            )

    return pl.pallas_call(
        kernel,
        grid_spec=pltpu.PrefetchScalarGridSpec(
            num_scalar_prefetch=1,
            grid=(sequences, n_ctx // blocks),
            in_specs=[
                pl.BlockSpec((blocks, 1, span, FUSED_GROUP), lambda s, i, n: (i, s, 0, 0)),
                pl.BlockSpec((n_ctx, 1, span, FUSED_GROUP), lambda s, i, n: (0, s, 0, 0)),
                pl.BlockSpec((blocks, 1, span, QUERY_GROUP), lambda s, i, n: (i, s, 0, 0)),
                pl.BlockSpec((tile, LANES), lambda s, i, n: (i, 0)),
                pl.BlockSpec((8, seq_len), lambda s, i, n: (0, 0)),
                pl.BlockSpec((seq_len, LANES), lambda s, i, n: (0, 0)),
                pl.BlockSpec((seq_len, LANES), lambda s, i, n: (0, 0)),
            ],
            out_specs=pl.BlockSpec((n_ctx, 1, span, FUSED_GROUP), lambda s, i, n: (0, s, 0, 0)),
            scratch_shapes=[
                pltpu.VMEM((seq_len, QUERY_GROUP), jnp.float32),
                pltpu.VMEM((seq_len, HEAD_DIM), jnp.float32),
                pltpu.VMEM((seq_len, HEAD_DIM), jnp.float32),
            ],
        ),
        out_shape=jax.ShapeDtypeStruct((n_ctx, sequences, span, FUSED_GROUP), jnp.bfloat16),
        name="attend_back",
        compiler_params=params(2),
    )(
        lengths_here,
        fused_rows,
        fused_rows,
        d_attended,
        row_positions,
        column_positions,
        cosine,
        sine_part,
    )


def project_out(attended_groups, rows_in, out_weight, gain_row):
    tokens, width = rows_in.shape

    def kernel(groups, rows, weight, gain, residual, normed, joined):
        attended = jnp.concatenate([groups[j] for j in range(KEY_VALUE_HEADS)], 1)
        joined[...] = attended
        total = rows[...].astype(jnp.float32) + plain(attended, weight[...])
        residual[...] = total
        normed[...] = (total * rms_scale(total) * gain[...]).astype(jnp.bfloat16)

    return pl.pallas_call(
        kernel,
        grid=(1,),
        in_specs=[
            whole(attended_groups.shape),
            whole((tokens, width)),
            whole((QUERY_HEADS * HEAD_DIM, width)),
            whole((1, width)),
        ],
        out_specs=[
            whole((tokens, width)),
            whole((tokens, width)),
            whole((tokens, QUERY_HEADS * HEAD_DIM)),
        ],
        out_shape=[
            jax.ShapeDtypeStruct((tokens, width), jnp.float32),
            jax.ShapeDtypeStruct((tokens, width), jnp.bfloat16),
            jax.ShapeDtypeStruct((tokens, QUERY_HEADS * HEAD_DIM), jnp.bfloat16),
        ],
        name="project_out",
        compiler_params=params(1),
    )(attended_groups, rows_in, out_weight, gain_row)


def expert_chunk(
    first_expert,
    expert_total,
    side,
    ctx_parts,
    normed_rows,
    normed_turned,
    cotangent_rows,
    cotangent_turned,
    gate_table,
    w_gate,
    w_up,
    w_down,
    kept,
    halves,
):
    rows, width = normed_rows.shape
    experts, _, hidden = w_gate.shape
    pair_width = 2 * hidden
    slab = width // (2 * ctx_parts)
    row_block = min(ROW_BLOCK, rows)

    def kernel(
        side_ref,
        normed,
        normed_t,
        cotan,
        cotan_t,
        gates,
        gate_w,
        up_w,
        down_w,
        *rest,
    ):
        grads, acts, d_gates = rest[-4 + (not halves) : -2], rest[-2], rest[-1]
        first = first_expert + 2 * pl.program_id(0)

        @pl.when(pl.program_id(0) == 0)
        def _():
            d_gates[...] = jnp.zeros_like(d_gates)

        def joined(pair_ref):
            return jnp.concatenate([pair_ref[0], pair_ref[1]], axis=1)

        gate_pair, up_pair, down_pair = joined(gate_w), joined(up_w), joined(down_w)
        lane = lax.broadcasted_iota(jnp.int32, (row_block, LANES), 1)

        def row_step(block, carry):
            span = pl.ds(pl.multiple_of(block * row_block, row_block), row_block)
            normed_part, cotan_part = normed[span, :], cotan[span, :]
            gate_part = gates[span, :]
            slot_gate = jnp.concatenate(
                [
                    jnp.broadcast_to(
                        jnp.sum(
                            jnp.where(lane == first + j, gate_part, 0.0), axis=1, keepdims=True
                        ),
                        (row_block, hidden),
                    )
                    for j in range(2)
                ],
                axis=1,
            )
            gate_pre = plain(normed_part, gate_pair)
            up_pre = plain(normed_part, up_pair)
            d_scaled = plain(cotan_part, down_pair)
            sigmoid_gate = jax.nn.sigmoid(gate_pre)
            silu_gate = gate_pre * sigmoid_gate
            scaled = (slot_gate * silu_gate * up_pre).astype(jnp.bfloat16)
            gate_term = d_scaled * silu_gate * up_pre
            d_gate_part = d_gates[span, :]
            for j in range(2):
                d_gate_part = d_gate_part + jnp.where(
                    lane == first + j,
                    jnp.sum(gate_term[:, j * hidden : (j + 1) * hidden], axis=1, keepdims=True),
                    0.0,
                )
            d_gates[span, :] = d_gate_part
            d_act = d_scaled * slot_gate
            acts[0, 0, span, :] = scaled
            acts[1, 0, span, :] = (
                d_act * up_pre * (sigmoid_gate + silu_gate * (1.0 - sigmoid_gate))
            ).astype(jnp.bfloat16)
            acts[2, 0, span, :] = (d_act * silu_gate).astype(jnp.bfloat16)
            return carry

        lax.fori_loop(0, rows // row_block, row_step, 0)
        for turn in range(2):
            choice = side_ref[0] if turn else 1 - side_ref[0]
            for kind, source in ((0, normed_t), (1, normed_t), (2, cotan_t)):
                if halves:
                    left_side = jnp.concatenate(
                        [
                            source[pl.ds(pl.multiple_of((2 * part + choice) * slab, 16), slab), :]
                            for part in range(ctx_parts)
                        ],
                        0,
                    )
                    target, base = grads[1 - turn], 0
                else:
                    base = turn * (width // 2)
                    left_side = source[base : base + width // 2, :]
                    target = grads[0]
                term = plain(left_side, acts[(1, 2, 0)[kind], 0]).astype(jnp.bfloat16)
                for j in range(2):
                    target[kind, j, base : base + width // 2, :] = term[
                        :, j * hidden : (j + 1) * hidden
                    ]

    start = first_expert // 2

    def weight_block():
        return pl.BlockSpec((2, width, hidden), lambda pair, side: (pair + start, 0, 0))

    grad_count = 2 if halves else 1
    grad_width = width // grad_count
    grad_block = pl.BlockSpec((3, 2, grad_width, hidden), lambda pair, side: (0, pair, 0, 0))
    grad_shape = jax.ShapeDtypeStruct((3, expert_total, grad_width, hidden), jnp.bfloat16)
    extra = [] if kept is None else [kept]
    return pl.pallas_call(
        kernel,
        grid_spec=pltpu.PrefetchScalarGridSpec(
            num_scalar_prefetch=1,
            grid=(expert_total // 2,),
            in_specs=[
                whole((rows, width)),
                whole((width, rows)),
                whole((rows, width)),
                whole((width, rows)),
                whole((rows, LANES)),
                weight_block(),
                weight_block(),
                weight_block(),
            ]
            + [pl.BlockSpec(memory_space=pl.ANY)] * len(extra),
            out_specs=[grad_block] * grad_count
            + [
                pl.BlockSpec(
                    (3, 1, rows, pair_width), lambda pair, side: (0, pair + start, 0, 0)
                ),
                whole((rows, LANES)),
            ],
        ),
        out_shape=[grad_shape] * grad_count
        + [
            jax.ShapeDtypeStruct((3, experts // 2, rows, pair_width), jnp.bfloat16),
            jax.ShapeDtypeStruct((rows, LANES), jnp.float32),
        ],
        input_output_aliases={9: grad_count} if extra else {},
        name="expert_chunk",
        compiler_params=params(1),
    )(
        side,
        normed_rows,
        normed_turned,
        cotangent_rows,
        cotangent_turned,
        gate_table,
        w_gate,
        w_up,
        w_down,
        *extra,
    )


def expert_rows(core, kinds, weights, acts, d_gates, route_hot):
    _, pairs, rows, pair_width = acts.shape
    _, width, hidden = weights[0].shape
    step_pairs = 4
    total = len(kinds)
    gate_lanes = 0 if d_gates is None else LANES
    row_block = rows // 4

    def kernel(core_ref, *refs):
        act_refs, weight_refs = refs[:total], refs[total : 2 * total]
        stay, leave, keep = refs[-3:]
        step = pl.program_id(0)
        right_side = jnp.concatenate(
            [ref[j] for ref in weight_refs for j in range(2 * step_pairs)], 1
        )
        for slot in range(4):
            target = leave if slot < 2 else stay
            choice = core_ref[0] if slot >= 2 else 1 - core_ref[0]
            span = pl.ds(
                pl.multiple_of((2 * (slot % 2) + choice) * row_block, row_block), row_block
            )
            left_side = jnp.concatenate(
                [ref[0, j, span, :] for ref in act_refs for j in range(step_pairs)], 1
            )
            term = turned(left_side, right_side)

            @pl.when(step == 0)
            def _():
                keep[span, :] = term

            @pl.when((step > 0) & (step < pl.num_programs(0) - 1))
            def _():
                keep[span, :] += term

            @pl.when(step == pl.num_programs(0) - 1)
            def _():
                target[slot % 2, :, :width] = (keep[span, :] + term).astype(jnp.bfloat16)
                if gate_lanes:
                    target[slot % 2, :, width:] = (
                        refs[2 * total][span, :] * refs[2 * total + 1][span, :]
                    ).astype(jnp.bfloat16)

    def act_block(kind):
        return pl.BlockSpec((1, step_pairs, rows, pair_width), lambda i, core: (kind, i, 0, 0))

    extra = [] if d_gates is None else [d_gates, route_hot]
    out_dims = (2, row_block, width + gate_lanes)
    return pl.pallas_call(
        kernel,
        grid_spec=pltpu.PrefetchScalarGridSpec(
            num_scalar_prefetch=1,
            grid=(pairs // step_pairs,),
            in_specs=[act_block(kind) for kind in kinds]
            + [pl.BlockSpec((2 * step_pairs, width, hidden), lambda i, core: (i, 0, 0))] * total
            + [whole((rows, LANES))] * len(extra),
            out_specs=[whole(out_dims)] * 2,
            scratch_shapes=[pltpu.VMEM((rows, width), jnp.float32)],
        ),
        out_shape=[jax.ShapeDtypeStruct(out_dims, jnp.bfloat16)] * 2,
        name="expert_rows",
        compiler_params=params(1),
    )(core, *([acts] * total), *weights, *extra)


def middle_back(
    d_kept, d_arrived, probs, share_row, live_lanes, residual, cotangent_rows, gain_row, weight
):
    tokens, width = residual.shape

    def kernel(
        kept_ref,
        arrived_ref,
        prob_ref,
        share_ref,
        live_ref,
        residual_ref,
        cotan_ref,
        gain_ref,
        weight_ref,
        d_residual,
        d_branch,
        d_logits,
        d_gain,
        d_groups,
    ):
        packed = kept_ref[...].astype(jnp.float32) + arrived_ref[...].astype(jnp.float32)
        prob = prob_ref[...]
        live = live_ref[...]
        d_prob = packed[:, width:] + share_ref[...] * live
        logits = (prob * (d_prob - jnp.sum(prob * d_prob, -1, keepdims=True))).astype(jnp.bfloat16)
        d_logits[...] = logits
        d_normed = packed[:, :width] + turned(logits, weight_ref[:, width:])
        total = residual_ref[...]
        scale = rms_scale(total)
        unit = total * scale
        d_gain[...] = jnp.broadcast_to(jnp.sum(d_normed * unit, 0, keepdims=True), (8, width))
        d_unit = d_normed * gain_ref[...]
        d_total = cotan_ref[...].astype(jnp.float32) * live[:, :1] + scale * (
            d_unit - unit * jnp.mean(d_unit * unit, -1, keepdims=True)
        )
        d_residual[...] = d_total
        low = d_total.astype(jnp.bfloat16)
        d_branch[...] = low
        for j in range(KEY_VALUE_HEADS):
            d_groups[j] = turned(
                low, weight_ref[j * QUERY_GROUP : (j + 1) * QUERY_GROUP, :width]
            ).astype(jnp.bfloat16)

    inputs = (d_kept, d_arrived, probs, share_row, live_lanes, residual, cotangent_rows, gain_row, weight)
    out_shape = [
        jax.ShapeDtypeStruct((tokens, width), jnp.float32),
        jax.ShapeDtypeStruct((tokens, width), jnp.bfloat16),
        jax.ShapeDtypeStruct((tokens, LANES), jnp.bfloat16),
        jax.ShapeDtypeStruct((8, width), jnp.float32),
        jax.ShapeDtypeStruct((KEY_VALUE_HEADS, tokens, QUERY_GROUP), jnp.bfloat16),
    ]
    return pl.pallas_call(
        kernel,
        grid=(1,),
        in_specs=[whole(value.shape) for value in inputs],
        out_specs=[whole(value.shape) for value in out_shape],
        out_shape=out_shape,
        name="middle_back",
        compiler_params=params(1),
    )(*inputs)


def early_grads(attended, d_branch, normed, d_logits, d_gain, gain_lane):
    tokens, width = normed.shape
    block = width // 3

    def kernel(attended_ref, branch_ref, normed_ref, logits_ref, gain_ref, out_ref):
        out_ref[:, :width] = over_rows(attended_ref[...], branch_ref[...]).astype(jnp.bfloat16)
        side_term = over_rows(normed_ref[...], logits_ref[...])
        column = jnp.broadcast_to(gain_ref[:1, :], (LANES, block)).T
        lane = lax.broadcasted_iota(jnp.int32, (block, LANES), 1)
        out_ref[:, width:] = jnp.where(lane == gain_lane, column, side_term).astype(jnp.bfloat16)

    return pl.pallas_call(
        kernel,
        grid=(3,),
        in_specs=[
            pl.BlockSpec((tokens, block), lambda i: (0, i)),
            whole((tokens, width)),
            pl.BlockSpec((tokens, block), lambda i: (0, i)),
            whole((tokens, LANES)),
            pl.BlockSpec((8, block), lambda i: (0, i)),
        ],
        out_specs=pl.BlockSpec((block, width + LANES), lambda i: (i, 0)),
        out_shape=jax.ShapeDtypeStruct((width, width + LANES), jnp.bfloat16),
        name="early_grads",
        compiler_params=params(1),
    )(attended, d_branch, normed, d_logits, d_gain)


def project_back(d_fused, fused_weight, normed, rows_in, gain_row, d_residual):
    tokens, width = rows_in.shape
    steps = KEY_VALUE_HEADS // 2
    query_step, head_step = 2 * QUERY_GROUP, 2 * HEAD_DIM
    key_start = KEY_VALUE_HEADS * QUERY_GROUP
    value_start = key_start + KEY_VALUE_HEADS * HEAD_DIM

    def kernel(
        d_ref, query_w, key_w, value_w, normed_ref, rows, gain, d_residual_ref, late, d_input, keep
    ):
        step = pl.program_id(0)
        first, second = d_ref[0], d_ref[1]
        key_end = QUERY_GROUP + HEAD_DIM
        d_pair = jnp.concatenate(
            [
                first[:, :QUERY_GROUP],
                second[:, :QUERY_GROUP],
                first[:, QUERY_GROUP:key_end],
                second[:, QUERY_GROUP:key_end],
                first[:, key_end:],
                second[:, key_end:],
            ],
            1,
        )
        grad = over_rows(normed_ref[...], d_pair).astype(jnp.bfloat16)
        late[:, pl.ds(pl.multiple_of(step * query_step, LANES), query_step)] = grad[:, :query_step]
        late[:, pl.ds(pl.multiple_of(key_start + step * head_step, LANES), head_step)] = grad[
            :, query_step : query_step + head_step
        ]
        late[:, pl.ds(pl.multiple_of(value_start + step * head_step, LANES), head_step)] = grad[
            :, query_step + head_step :
        ]
        term = turned(d_pair, jnp.concatenate([query_w[...], key_w[...], value_w[...]], 1))

        @pl.when(step == 0)
        def _():
            keep[...] = term

        @pl.when(step > 0)
        def _():
            keep[...] += term

        @pl.when(step == steps - 1)
        def _():
            values = rows[...].astype(jnp.float32)
            scale = rms_scale(values)
            unit = values * scale
            d_normed = keep[...]
            d_unit = d_normed * gain[...]
            d_input[...] = d_residual_ref[...] + scale * (
                d_unit - unit * jnp.mean(d_unit * unit, -1, keepdims=True)
            )
            d_gain = jnp.sum(d_normed * unit, 0, keepdims=True)
            late[:, FUSED_WIDTH:] = jnp.broadcast_to(d_gain, (LANES, width)).T.astype(jnp.bfloat16)

    return pl.pallas_call(
        kernel,
        grid=(steps,),
        in_specs=[
            pl.BlockSpec((2, tokens, FUSED_GROUP), lambda i: (i, 0, 0)),
            pl.BlockSpec((width, query_step), lambda i: (0, i)),
            pl.BlockSpec((width, head_step), lambda i: (0, key_start // head_step + i)),
            pl.BlockSpec((width, head_step), lambda i: (0, value_start // head_step + i)),
            whole((tokens, width)),
            whole((tokens, width)),
            whole((1, width)),
            whole((tokens, width)),
        ],
        out_specs=[whole((width, FUSED_WIDTH + LANES)), whole((tokens, width))],
        out_shape=[
            jax.ShapeDtypeStruct((width, FUSED_WIDTH + LANES), jnp.bfloat16),
            jax.ShapeDtypeStruct((tokens, width), jnp.float32),
        ],
        scratch_shapes=[pltpu.VMEM((tokens, width), jnp.float32)],
        name="project_back",
        compiler_params=params(1),
    )(d_fused, fused_weight, fused_weight, fused_weight, normed, rows_in, gain_row, d_residual)


def body(
    layer_input,
    gain_attn,
    w_query,
    key_projection_weight,
    value_projection_weight,
    w_out,
    gain_ffn,
    w_router,
    w_gate,
    w_up,
    w_down,
    routes,
    lengths,
    cotangent,
):
    ctx_parts = lax.axis_size("z")
    n_ctx = 2 * ctx_parts
    n_shard = 2 * lax.axis_size("x")
    ctx_side = lax.axis_index("y")
    ctx_pos = 2 * lax.axis_index("z") + ctx_side
    shard_pos = 2 * lax.axis_index("x") + lax.axis_index("k")
    local_sequences = layer_input.shape[0]
    half_rows = layer_input.shape[3]
    model_width = layer_input.shape[4]
    sequence_rows = 2 * half_rows
    tokens = local_sequences * sequence_rows
    seq_len = n_ctx * sequence_rows
    experts = w_gate.shape[0]
    top_k = routes.shape[4]
    gathered_rows = n_shard * tokens
    head_shares = n_ctx // KEY_VALUE_HEADS
    here_sequences = local_sequences // head_shares
    width_rows = gain_attn.shape[0]

    core_pos = lax.axis_index("k")
    chip_pos = lax.axis_index("x")
    swap = [(0, 1), (1, 0)]

    def added(first, second):
        return (first.astype(jnp.float32) + second.astype(jnp.float32)).astype(jnp.bfloat16)

    def picked(values, which):
        return lax.dynamic_index_in_dim(values, which, 0, keepdims=False)

    def chip_halves(stay, arrived):
        leave_now = added(picked(stay, 1 - chip_pos), picked(arrived, 1 - chip_pos))
        return (
            added(picked(stay, chip_pos), picked(arrived, chip_pos)),
            lax.ppermute(leave_now, "x", swap),
        )

    def halved_by(values, axis_name, which):
        return added(
            picked(values, which), lax.ppermute(picked(values, 1 - which), axis_name, swap)
        )

    def reduced_rows(terms):
        columns = terms.shape[1]
        parts = terms.reshape(ctx_parts, 2, 2, 2, -1, columns)
        for axis_name, which, dim in (("k", core_pos, 3), ("x", chip_pos, 2), ("y", ctx_side, 1)):
            parts = halved_by(jnp.moveaxis(parts, dim, 0), axis_name, which)
        return lax.psum_scatter(
            parts.reshape(-1, columns), "z", scatter_dimension=0, tiled=True
        ).astype(jnp.float32)

    fused_weight = lax.all_gather(
        jnp.concatenate(
            [
                w_query,
                key_projection_weight,
                value_projection_weight,
                jnp.pad(gain_attn[:, None], ((0, 0), (0, LANES - 1))),
            ],
            1,
        ),
        SHARD,
        axis=0,
        tiled=True,
    )
    out_weight = lax.all_gather(
        jnp.concatenate(
            [
                w_out,
                w_router,
                gain_ffn[:, None],
                jnp.zeros((width_rows, LANES - experts - 1), jnp.bfloat16),
            ],
            1,
        ),
        SHARD,
        axis=0,
        tiled=True,
    )
    gain_one = fused_weight[:, FUSED_WIDTH].astype(jnp.float32)[None, :]
    gain_two = out_weight[:, model_width + experts].astype(jnp.float32)[None, :]
    router_matrix = out_weight[:, model_width : model_width + experts]

    slots = jnp.arange(seq_len, dtype=jnp.int32)
    slot_ctx, slot_row = slots // sequence_rows, slots % sequence_rows
    all_positions = (
        jnp.where(slot_row < half_rows, slot_ctx, 2 * n_ctx - 1 - slot_ctx) * half_rows
        + slot_row % half_rows
    )
    local_positions = lax.dynamic_slice_in_dim(all_positions, ctx_pos * sequence_rows, sequence_rows)
    seq_lengths = lax.dynamic_slice_in_dim(lengths, shard_pos * local_sequences, local_sequences)
    lengths_here = lax.dynamic_slice_in_dim(
        seq_lengths, (ctx_pos % head_shares) * here_sequences, here_sequences
    )
    live_rows = (local_positions[None, :] < seq_lengths[:, None]).reshape(tokens)
    live_lanes = jnp.broadcast_to(live_rows.astype(jnp.float32)[:, None], (tokens, LANES))
    live_group = (
        (local_positions[None, :] < lengths[:, None]).astype(jnp.float32).reshape(gathered_rows)
    )
    row_positions = jnp.broadcast_to(all_positions[:, None], (seq_len, LANES))
    column_positions = jnp.broadcast_to(all_positions[None, :], (8, seq_len))
    every_cos, every_sin = rope_tables(all_positions)
    own_cos, own_sin = rope_tables(local_positions)
    step_cos = jnp.tile(own_cos, (local_sequences, 2 * (GROUP + 1)))
    step_sin = jnp.tile(own_sin, (local_sequences, 2 * (GROUP + 1)))
    pair_cos, pair_sin = jnp.tile(every_cos, (1, 2)), jnp.tile(every_sin, (1, 2))

    rows_in = layer_input.reshape(tokens, model_width)
    cotangent_rows = cotangent.reshape(tokens, model_width)
    d_moe = jnp.where(live_rows[:, None], cotangent_rows, jnp.bfloat16(0.0))
    d_moe_all = lax.all_gather(d_moe, SHARD, axis=0, tiled=True)
    d_moe_turned = d_moe_all.T

    def exchange(groups):
        return lax.all_to_all(groups, CTX, 0, 0, tiled=True)

    fused_own, first_normed = project_in(rows_in, gain_one, fused_weight, step_cos, step_sin)
    fused_rows = exchange(
        fused_own.reshape(n_ctx, here_sequences, sequence_rows, FUSED_GROUP)
    )
    attended_rows = attend(fused_rows, row_positions, column_positions, lengths_here)
    attended_groups = exchange(attended_rows).reshape(KEY_VALUE_HEADS, tokens, QUERY_GROUP)
    residual, second_normed, attended_low = project_out(
        attended_groups, rows_in, out_weight, gain_two
    )

    normed_all = lax.all_gather(second_normed, SHARD, axis=0, tiled=True)
    normed_turned = normed_all.T
    router_probs = jax.nn.softmax(plain(normed_all, router_matrix), axis=-1)
    route_hot = jnp.any(
        routes.reshape(gathered_rows, top_k, 1) == jnp.arange(experts, dtype=jnp.int32), axis=1
    ).astype(jnp.float32)
    lane_pad = ((0, 0), (0, LANES - experts))
    prob_table = jnp.pad(router_probs, lane_pad)
    hot_table = jnp.pad(route_hot, lane_pad)
    gate_table = prob_table * hot_table

    group_sums = jnp.concatenate(
        [
            jnp.sum(hot_table * live_group[:, None], 0, keepdims=True),
            jnp.sum(prob_table * live_group[:, None], 0, keepdims=True),
        ],
        0,
    )
    for axis_name, count in (("y", 2), ("z", ctx_parts)):
        step = 1
        while step < count:
            group_sums = group_sums + lax.ppermute(
                group_sums, axis_name, [(i, i ^ step) for i in range(count)]
            )
            step *= 2
    all_sums = group_sums[:, :experts]

    side = ctx_side.astype(jnp.int32).reshape(1)
    core = core_pos.astype(jnp.int32).reshape(1)
    acts, d_gates, reduced = None, None, []
    first_expert = 0
    for number, chunk in enumerate(CHUNKS):
        *terms, acts, gate_piece = expert_chunk(
            first_expert,
            chunk,
            side,
            ctx_parts,
            normed_all,
            normed_turned,
            d_moe_all,
            d_moe_turned,
            gate_table,
            w_gate,
            w_up,
            w_down,
            acts,
            number > 0,
        )
        first_expert += chunk
        d_gates = gate_piece if d_gates is None else d_gates + gate_piece
        if number:
            arrived = lax.ppermute(terms[1], "y", swap)
            halved = added(terms[0], arrived)
            if number == 1:
                first_halved = halved
            if number == 2:
                second_halved = halved
            reduced.append(lax.psum_scatter(halved, "z", scatter_dimension=2, tiled=True))
        else:
            ringed = lax.psum_scatter(terms[0], "z", scatter_dimension=2, tiled=True)

    acts, first_halved = lax.optimization_barrier((acts, first_halved))
    d_stay, d_leave = expert_rows(core, (1, 2), (w_gate, w_up), acts, d_gates, hot_table)
    d_came = lax.ppermute(d_leave, "k", swap)
    d_kept, d_arrived = chip_halves(d_stay, d_came)
    moe_stay, moe_leave = expert_rows(core, (0,), (w_down,), acts, None, None)
    moe_kept, moe_arrived = chip_halves(moe_stay, lax.ppermute(moe_leave, "k", swap))
    layer_output = (
        (residual + moe_kept.astype(jnp.float32) + moe_arrived.astype(jnp.float32))
        .astype(jnp.bfloat16)
        .reshape(layer_input.shape)
    )
    ringed = jnp.moveaxis(
        ringed.reshape(3, CHUNKS[0], 2, model_width // n_ctx, -1), 2, 0
    )
    reduced.insert(0, halved_by(ringed, "y", ctx_side))

    live_all = jnp.sum(lengths).astype(jnp.float32)
    route_share = all_sums[0] / (top_k * live_all)
    aux_loss = experts * jnp.sum(route_share * all_sums[1] / live_all)
    share_row = jnp.pad((loss_weight * experts / live_all) * route_share[None, :], lane_pad)

    own_probs = lax.dynamic_slice_in_dim(prob_table, shard_pos * tokens, tokens, 0)
    d_residual, d_branch, d_logits, d_gain_two, d_groups = middle_back(
        d_kept,
        d_arrived,
        own_probs,
        share_row,
        live_lanes,
        residual,
        cotangent_rows,
        gain_two,
        out_weight,
    )
    d_attended = exchange(d_groups.reshape(n_ctx, here_sequences, sequence_rows, QUERY_GROUP))
    d_branch, d_attended, second_halved = lax.optimization_barrier(
        (d_branch, d_attended, second_halved)
    )
    early_terms = early_grads(attended_low, d_branch, second_normed, d_logits, d_gain_two, experts)
    d_fused_rows = attend_back(
        fused_rows,
        d_attended,
        row_positions,
        column_positions,
        pair_cos,
        pair_sin,
        lengths_here,
    )
    d_fused = exchange(d_fused_rows).reshape(KEY_VALUE_HEADS, tokens, FUSED_GROUP)
    late_terms, grad_input = project_back(
        d_fused, fused_weight, first_normed, rows_in, gain_one, d_residual
    )
    early_rows, late_rows = reduced_rows(early_terms), reduced_rows(late_terms)
    query_end = KEY_VALUE_HEADS * QUERY_GROUP
    key_end = query_end + KEY_VALUE_HEADS * HEAD_DIM
    grads = [
        jnp.concatenate([piece[kind] for piece in reduced], 0).astype(jnp.float32)
        for kind in range(3)
    ]
    return (
        layer_output,
        grad_input.reshape(layer_input.shape),
        late_rows[:, FUSED_WIDTH],
        late_rows[:, :query_end],
        late_rows[:, query_end:key_end],
        late_rows[:, key_end:FUSED_WIDTH],
        early_rows[:, :model_width],
        early_rows[:, model_width + experts],
        early_rows[:, model_width : model_width + experts],
        grads[0],
        grads[1],
        grads[2],
        aux_loss,
    )


def solution(mesh):
    n_ctx, n_shard = mesh.shape["ctx"], mesh.shape["fsdp"]
    fine = Mesh(mesh.devices.reshape(n_ctx // 2, 2, n_shard // 2, 2), EVERY)
    placed = (
        P(SHARD, CTX, None, None, None),
        P(SHARD),
        P(SHARD, None),
        P(SHARD, None),
        P(SHARD, None),
        P(SHARD, None),
        P(SHARD),
        P(SHARD, None),
        P(None, None, SHARD),
        P(None, None, SHARD),
        P(None, None, SHARD),
        P(None, CTX, None, None, None),
        P(),
        P(SHARD, CTX, None, None, None),
    )
    return jax.shard_map(
        body,
        mesh=fine,
        in_specs=placed,
        out_specs=(
            P(SHARD, CTX, None, None, None),
            P(SHARD, CTX, None, None, None),
            P(EVERY),
            P(EVERY, None),
            P(EVERY, None),
            P(EVERY, None),
            P(EVERY, None),
            P(EVERY),
            P(EVERY, None),
            P(None, CTX, SHARD),
            P(None, CTX, SHARD),
            P(None, CTX, SHARD),
            P(),
        ),
        check_vma=False,
    )
```

```python
import jax
import jax.numpy as jnp
from jax import lax
from jax.experimental import pallas as pl
from jax.experimental.pallas import tpu as pltpu
from jax.sharding import Mesh
from jax.sharding import PartitionSpec as P


QUERY_HEADS = 24
KEY_VALUE_HEADS = 8
HEAD_DIM = 64
GROUP = QUERY_HEADS // KEY_VALUE_HEADS
QUERY_GROUP = GROUP * HEAD_DIM
FUSED_GROUP = QUERY_GROUP + 2 * HEAD_DIM
FUSED_WIDTH = KEY_VALUE_HEADS * FUSED_GROUP
LANES = 128
ROW_BLOCK = 512
CHUNKS = (8, 8, 8, 4, 8, 4)
CTX = ("z", "y")
SHARD = ("x", "k")
EVERY = ("z", "y", "x", "k")

epsilon = 1e-05
rope_base = 10000.0
loss_weight = 0.01
mask_value = -1e30


def plain(left_side, right_side):
    return jnp.dot(left_side, right_side, preferred_element_type=jnp.float32)


def turned(left_side, right_side):
    return lax.dot_general(
        left_side, right_side, (((1,), (1,)), ((), ())), preferred_element_type=jnp.float32
    )


def over_rows(left_side, right_side):
    return lax.dot_general(
        left_side, right_side, (((0,), (0,)), ((), ())), preferred_element_type=jnp.float32
    )


def rms_scale(values):
    return lax.rsqrt(jnp.mean(values * values, -1, keepdims=True) + epsilon)


def params(count):
    return pltpu.CompilerParams(
        dimension_semantics=("arbitrary",) * count, vmem_limit_bytes=60 * 1024 * 1024
    )


def whole(shape, single=True):
    zeros = (0,) * len(shape)
    if single:
        return pl.BlockSpec(shape, lambda *ids: zeros, pipeline_mode=pl.Buffered(1))
    return pl.BlockSpec(shape, lambda *ids: zeros)


def rope_tables(token_positions):
    frequency = rope_base ** (-jnp.arange(HEAD_DIM // 2, dtype=jnp.float32) * 2.0 / HEAD_DIM)
    angles = token_positions.astype(jnp.float32)[..., None] * frequency
    cosine, sine_part = jnp.cos(angles), jnp.sin(angles)
    return (
        jnp.concatenate([cosine, cosine], -1),
        jnp.concatenate([-sine_part, sine_part], -1),
    )


def swapped_halves(values):
    width = values.shape[1]
    lane = lax.broadcasted_iota(jnp.int32, values.shape, 1)
    ahead = pltpu.roll(values, width - HEAD_DIM // 2, 1)
    behind = pltpu.roll(values, HEAD_DIM // 2, 1)
    return jnp.where(lane % HEAD_DIM < HEAD_DIM // 2, ahead, behind)


def project_in(rows_in, gain_row, fused_weight, cosine, sine_part):
    tokens, width = rows_in.shape
    query_step, head_step = 2 * QUERY_GROUP, 2 * HEAD_DIM
    rotated_width = query_step + head_step

    def kernel(rows, gain, query_w, key_w, value_w, cos_ref, sin_ref, fused, normed):
        @pl.when(pl.program_id(0) == 0)
        def _():
            values = rows[...].astype(jnp.float32)
            normed[...] = (values * rms_scale(values) * gain[...]).astype(jnp.bfloat16)

        product = plain(
            normed[...], jnp.concatenate([query_w[...], key_w[...], value_w[...]], 1)
        )
        turning = product[:, :rotated_width]
        rotated = (turning * cos_ref[...] + swapped_halves(turning) * sin_ref[...]).astype(
            jnp.bfloat16
        )
        values_low = product[:, rotated_width:].astype(jnp.bfloat16)
        for j in range(2):
            lanes = slice(j * HEAD_DIM, (j + 1) * HEAD_DIM)
            fused[j] = jnp.concatenate(
                [
                    rotated[:, j * QUERY_GROUP : (j + 1) * QUERY_GROUP],
                    rotated[:, query_step:][:, lanes],
                    values_low[:, lanes],
                ],
                1,
            )

    key_start = KEY_VALUE_HEADS * QUERY_GROUP // head_step
    value_start = key_start + KEY_VALUE_HEADS // 2
    return pl.pallas_call(
        kernel,
        grid=(KEY_VALUE_HEADS // 2,),
        in_specs=[
            whole((tokens, width)),
            whole((1, width)),
            pl.BlockSpec((width, query_step), lambda i: (0, i)),
            pl.BlockSpec((width, head_step), lambda i: (0, key_start + i)),
            pl.BlockSpec((width, head_step), lambda i: (0, value_start + i)),
            whole((tokens, rotated_width)),
            whole((tokens, rotated_width)),
        ],
        out_specs=[
            pl.BlockSpec((2, tokens, FUSED_GROUP), lambda i: (i, 0, 0)),
            whole((tokens, width)),
        ],
        out_shape=[
            jax.ShapeDtypeStruct((KEY_VALUE_HEADS, tokens, FUSED_GROUP), jnp.bfloat16),
            jax.ShapeDtypeStruct((tokens, width), jnp.bfloat16),
        ],
        name="project_in",
        compiler_params=params(1),
    )(rows_in, gain_row, fused_weight, fused_weight, fused_weight, cosine, sine_part)


def head_probs(query_head, key_rows, visible):
    scores = jnp.where(visible, turned(query_head, key_rows) * HEAD_DIM ** (-0.5), mask_value)
    weights = jnp.exp(scores - jnp.max(scores, -1, keepdims=True))
    return weights * (1.0 / jnp.sum(weights, -1, keepdims=True))


def attend(fused_rows, row_positions, column_positions, lengths_here):
    n_ctx, sequences, span, _ = fused_rows.shape
    seq_len = n_ctx * span
    blocks = max(1, min(n_ctx, 512 * 512 // seq_len // span))
    tile = blocks * span

    def kernel(lengths_ref, query_ref, key_ref, row_ref, column_ref, out_ref):
        length = lengths_ref[pl.program_id(0)]
        fused_keys = key_ref[...].reshape(seq_len, FUSED_GROUP)
        key_rows = fused_keys[:, QUERY_GROUP : QUERY_GROUP + HEAD_DIM]
        value_rows = fused_keys[:, QUERY_GROUP + HEAD_DIM :]
        queries = query_ref[...].reshape(tile, FUSED_GROUP)
        key_pos = column_ref[:1, :]
        visible = (key_pos <= row_ref[:, :1]) & (key_pos < length)
        outs = []
        for head in range(GROUP):
            prob = head_probs(queries[:, head * HEAD_DIM : (head + 1) * HEAD_DIM], key_rows, visible)
            outs.append(plain(prob.astype(jnp.bfloat16), value_rows).astype(jnp.bfloat16))
        out_ref[...] = jnp.concatenate(outs, 1).reshape(blocks, 1, span, QUERY_GROUP)

    return pl.pallas_call(
        kernel,
        grid_spec=pltpu.PrefetchScalarGridSpec(
            num_scalar_prefetch=1,
            grid=(sequences, n_ctx // blocks),
            in_specs=[
                pl.BlockSpec((blocks, 1, span, FUSED_GROUP), lambda s, i, n: (i, s, 0, 0)),
                pl.BlockSpec((n_ctx, 1, span, FUSED_GROUP), lambda s, i, n: (0, s, 0, 0)),
                pl.BlockSpec((tile, LANES), lambda s, i, n: (i, 0)),
                pl.BlockSpec((8, seq_len), lambda s, i, n: (0, 0)),
            ],
            out_specs=pl.BlockSpec((blocks, 1, span, QUERY_GROUP), lambda s, i, n: (i, s, 0, 0)),
        ),
        out_shape=jax.ShapeDtypeStruct((n_ctx, sequences, span, QUERY_GROUP), jnp.bfloat16),
        name="attend",
        compiler_params=params(2),
    )(lengths_here, fused_rows, fused_rows, row_positions, column_positions)


def attend_back(
    fused_rows, d_attended, row_positions, column_positions, cosine, sine_part, lengths_here
):
    n_ctx, sequences, span, _ = fused_rows.shape
    seq_len = n_ctx * span
    blocks = max(1, min(n_ctx, 512 * 512 // seq_len // span))
    tile = blocks * span

    def kernel(
        lengths_ref,
        query_ref,
        key_ref,
        d_ref,
        row_ref,
        column_ref,
        cos_ref,
        sin_ref,
        out_ref,
        d_query_keep,
        d_key_keep,
        d_value_keep,
    ):
        part = pl.program_id(1)
        length = lengths_ref[pl.program_id(0)]
        fused_keys = key_ref[...].reshape(seq_len, FUSED_GROUP)
        key_rows = fused_keys[:, QUERY_GROUP : QUERY_GROUP + HEAD_DIM]
        value_rows = fused_keys[:, QUERY_GROUP + HEAD_DIM :]
        queries = query_ref[...].reshape(tile, FUSED_GROUP)
        d_rows = d_ref[...].reshape(tile, QUERY_GROUP)
        key_pos = column_ref[:1, :]
        visible = (key_pos <= row_ref[:, :1]) & (key_pos < length)

        @pl.when(part == 0)
        def _():
            d_key_keep[...] = jnp.zeros_like(d_key_keep)
            d_value_keep[...] = jnp.zeros_like(d_value_keep)

        d_queries = []
        for head in range(GROUP):
            lanes = slice(head * HEAD_DIM, (head + 1) * HEAD_DIM)
            query_head, d_head = queries[:, lanes], d_rows[:, lanes]
            prob = head_probs(query_head, key_rows, visible)
            d_prob = turned(d_head, value_rows)
            delta = jnp.sum(prob * d_prob, -1, keepdims=True)
            d_score = (prob * (d_prob - delta) * HEAD_DIM ** (-0.5)).astype(jnp.bfloat16)
            d_queries.append(plain(d_score, key_rows))
            d_key_keep[...] += over_rows(d_score, query_head)
            d_value_keep[...] += over_rows(prob.astype(jnp.bfloat16), d_head)
        d_query_keep[pl.ds(pl.multiple_of(part * tile, tile), tile), :] = jnp.concatenate(
            d_queries, 1
        )

        @pl.when(part == pl.num_programs(1) - 1)
        def _():
            turned_part = jnp.concatenate([d_query_keep[...], d_key_keep[...]], 1)
            table_cos = jnp.concatenate([cos_ref[...], cos_ref[...]], 1)
            table_sin = jnp.concatenate([sin_ref[...], sin_ref[...]], 1)
            back = turned_part * table_cos - swapped_halves(turned_part) * table_sin
            out_ref[...] = (
                jnp.concatenate([back, d_value_keep[...]], 1)
                .astype(jnp.bfloat16)
                .reshape(n_ctx, 1, span, FUSED_GROUP)
            )

    return pl.pallas_call(
        kernel,
        grid_spec=pltpu.PrefetchScalarGridSpec(
            num_scalar_prefetch=1,
            grid=(sequences, n_ctx // blocks),
            in_specs=[
                pl.BlockSpec((blocks, 1, span, FUSED_GROUP), lambda s, i, n: (i, s, 0, 0)),
                pl.BlockSpec((n_ctx, 1, span, FUSED_GROUP), lambda s, i, n: (0, s, 0, 0)),
                pl.BlockSpec((blocks, 1, span, QUERY_GROUP), lambda s, i, n: (i, s, 0, 0)),
                pl.BlockSpec((tile, LANES), lambda s, i, n: (i, 0)),
                pl.BlockSpec((8, seq_len), lambda s, i, n: (0, 0)),
                pl.BlockSpec((seq_len, LANES), lambda s, i, n: (0, 0)),
                pl.BlockSpec((seq_len, LANES), lambda s, i, n: (0, 0)),
            ],
            out_specs=pl.BlockSpec((n_ctx, 1, span, FUSED_GROUP), lambda s, i, n: (0, s, 0, 0)),
            scratch_shapes=[
                pltpu.VMEM((seq_len, QUERY_GROUP), jnp.float32),
                pltpu.VMEM((seq_len, HEAD_DIM), jnp.float32),
                pltpu.VMEM((seq_len, HEAD_DIM), jnp.float32),
            ],
        ),
        out_shape=jax.ShapeDtypeStruct((n_ctx, sequences, span, FUSED_GROUP), jnp.bfloat16),
        name="attend_back",
        compiler_params=params(2),
    )(
        lengths_here,
        fused_rows,
        fused_rows,
        d_attended,
        row_positions,
        column_positions,
        cosine,
        sine_part,
    )


def project_out(attended_groups, rows_in, out_weight, gain_row):
    tokens, width = rows_in.shape

    def kernel(groups, rows, weight, gain, residual, normed, joined):
        attended = jnp.concatenate([groups[j] for j in range(KEY_VALUE_HEADS)], 1)
        joined[...] = attended
        total = rows[...].astype(jnp.float32) + plain(attended, weight[...])
        residual[...] = total
        normed[...] = (total * rms_scale(total) * gain[...]).astype(jnp.bfloat16)

    return pl.pallas_call(
        kernel,
        grid=(1,),
        in_specs=[
            whole(attended_groups.shape),
            whole((tokens, width)),
            whole((QUERY_HEADS * HEAD_DIM, width)),
            whole((1, width)),
        ],
        out_specs=[
            whole((tokens, width)),
            whole((tokens, width)),
            whole((tokens, QUERY_HEADS * HEAD_DIM)),
        ],
        out_shape=[
            jax.ShapeDtypeStruct((tokens, width), jnp.float32),
            jax.ShapeDtypeStruct((tokens, width), jnp.bfloat16),
            jax.ShapeDtypeStruct((tokens, QUERY_HEADS * HEAD_DIM), jnp.bfloat16),
        ],
        name="project_out",
        compiler_params=params(1),
    )(attended_groups, rows_in, out_weight, gain_row)


def expert_chunk(
    first_expert,
    expert_total,
    side,
    ctx_parts,
    normed_rows,
    normed_turned,
    cotangent_rows,
    cotangent_turned,
    gate_table,
    w_gate,
    w_up,
    w_down,
    kept,
    halves,
):
    rows, width = normed_rows.shape
    experts, _, hidden = w_gate.shape
    pair_width = 2 * hidden
    slab = width // (2 * ctx_parts)
    row_block = min(ROW_BLOCK, rows)

    def kernel(
        side_ref,
        normed,
        normed_t,
        cotan,
        cotan_t,
        gates,
        gate_w,
        up_w,
        down_w,
        *rest,
    ):
        grads, acts, d_gates = rest[-4 + (not halves) : -2], rest[-2], rest[-1]
        first = first_expert + 2 * pl.program_id(0)

        @pl.when(pl.program_id(0) == 0)
        def _():
            d_gates[...] = jnp.zeros_like(d_gates)

        def joined(pair_ref):
            return jnp.concatenate([pair_ref[0], pair_ref[1]], axis=1)

        gate_pair, up_pair, down_pair = joined(gate_w), joined(up_w), joined(down_w)
        lane = lax.broadcasted_iota(jnp.int32, (row_block, LANES), 1)

        def row_step(block, carry):
            span = pl.ds(pl.multiple_of(block * row_block, row_block), row_block)
            normed_part, cotan_part = normed[span, :], cotan[span, :]
            gate_part = gates[span, :]
            slot_gate = jnp.concatenate(
                [
                    jnp.broadcast_to(
                        jnp.sum(
                            jnp.where(lane == first + j, gate_part, 0.0), axis=1, keepdims=True
                        ),
                        (row_block, hidden),
                    )
                    for j in range(2)
                ],
                axis=1,
            )
            gate_pre = plain(normed_part, gate_pair)
            up_pre = plain(normed_part, up_pair)
            d_scaled = plain(cotan_part, down_pair)
            sigmoid_gate = jax.nn.sigmoid(gate_pre)
            silu_gate = gate_pre * sigmoid_gate
            scaled = (slot_gate * silu_gate * up_pre).astype(jnp.bfloat16)
            gate_term = d_scaled * silu_gate * up_pre
            d_gate_part = d_gates[span, :]
            for j in range(2):
                d_gate_part = d_gate_part + jnp.where(
                    lane == first + j,
                    jnp.sum(gate_term[:, j * hidden : (j + 1) * hidden], axis=1, keepdims=True),
                    0.0,
                )
            d_gates[span, :] = d_gate_part
            d_act = d_scaled * slot_gate
            acts[0, 0, span, :] = scaled
            acts[1, 0, span, :] = (
                d_act * up_pre * (sigmoid_gate + silu_gate * (1.0 - sigmoid_gate))
            ).astype(jnp.bfloat16)
            acts[2, 0, span, :] = (d_act * silu_gate).astype(jnp.bfloat16)
            return carry

        lax.fori_loop(0, rows // row_block, row_step, 0)
        for turn in range(2):
            choice = side_ref[0] if turn else 1 - side_ref[0]
            for kind, source in ((0, normed_t), (1, normed_t), (2, cotan_t)):
                if halves:
                    left_side = jnp.concatenate(
                        [
                            source[pl.ds(pl.multiple_of((2 * part + choice) * slab, 16), slab), :]
                            for part in range(ctx_parts)
                        ],
                        0,
                    )
                    target, base = grads[1 - turn], 0
                else:
                    base = turn * (width // 2)
                    left_side = source[base : base + width // 2, :]
                    target = grads[0]
                term = plain(left_side, acts[(1, 2, 0)[kind], 0]).astype(jnp.bfloat16)
                for j in range(2):
                    target[kind, j, base : base + width // 2, :] = term[
                        :, j * hidden : (j + 1) * hidden
                    ]

    start = first_expert // 2

    def weight_block():
        return pl.BlockSpec((2, width, hidden), lambda pair, side: (pair + start, 0, 0))

    grad_count = 2 if halves else 1
    grad_width = width // grad_count
    grad_block = pl.BlockSpec((3, 2, grad_width, hidden), lambda pair, side: (0, pair, 0, 0))
    grad_shape = jax.ShapeDtypeStruct((3, expert_total, grad_width, hidden), jnp.bfloat16)
    extra = [] if kept is None else [kept]
    return pl.pallas_call(
        kernel,
        grid_spec=pltpu.PrefetchScalarGridSpec(
            num_scalar_prefetch=1,
            grid=(expert_total // 2,),
            in_specs=[
                whole((rows, width)),
                whole((width, rows)),
                whole((rows, width)),
                whole((width, rows)),
                whole((rows, LANES)),
                weight_block(),
                weight_block(),
                weight_block(),
            ]
            + [pl.BlockSpec(memory_space=pl.ANY)] * len(extra),
            out_specs=[grad_block] * grad_count
            + [
                pl.BlockSpec(
                    (3, 1, rows, pair_width), lambda pair, side: (0, pair + start, 0, 0)
                ),
                whole((rows, LANES)),
            ],
        ),
        out_shape=[grad_shape] * grad_count
        + [
            jax.ShapeDtypeStruct((3, experts // 2, rows, pair_width), jnp.bfloat16),
            jax.ShapeDtypeStruct((rows, LANES), jnp.float32),
        ],
        input_output_aliases={9: grad_count} if extra else {},
        name="expert_chunk",
        compiler_params=params(1),
    )(
        side,
        normed_rows,
        normed_turned,
        cotangent_rows,
        cotangent_turned,
        gate_table,
        w_gate,
        w_up,
        w_down,
        *extra,
    )


def expert_rows(core, kinds, weights, acts, d_gates, route_hot):
    _, pairs, rows, pair_width = acts.shape
    _, width, hidden = weights[0].shape
    step_pairs = 4
    total = len(kinds)
    gate_lanes = 0 if d_gates is None else LANES
    row_block = rows // 4

    def kernel(core_ref, *refs):
        act_refs, weight_refs = refs[:total], refs[total : 2 * total]
        stay, leave, keep = refs[-3:]
        step = pl.program_id(0)
        right_side = jnp.concatenate(
            [ref[j] for ref in weight_refs for j in range(2 * step_pairs)], 1
        )
        for slot in range(4):
            target = leave if slot < 2 else stay
            choice = core_ref[0] if slot >= 2 else 1 - core_ref[0]
            span = pl.ds(
                pl.multiple_of((2 * (slot % 2) + choice) * row_block, row_block), row_block
            )
            left_side = jnp.concatenate(
                [ref[0, j, span, :] for ref in act_refs for j in range(step_pairs)], 1
            )
            term = turned(left_side, right_side)

            @pl.when(step == 0)
            def _():
                keep[span, :] = term

            @pl.when((step > 0) & (step < pl.num_programs(0) - 1))
            def _():
                keep[span, :] += term

            @pl.when(step == pl.num_programs(0) - 1)
            def _():
                target[slot % 2, :, :width] = (keep[span, :] + term).astype(jnp.bfloat16)
                if gate_lanes:
                    target[slot % 2, :, width:] = (
                        refs[2 * total][span, :] * refs[2 * total + 1][span, :]
                    ).astype(jnp.bfloat16)

    def act_block(kind):
        return pl.BlockSpec((1, step_pairs, rows, pair_width), lambda i, core: (kind, i, 0, 0))

    extra = [] if d_gates is None else [d_gates, route_hot]
    out_dims = (2, row_block, width + gate_lanes)
    return pl.pallas_call(
        kernel,
        grid_spec=pltpu.PrefetchScalarGridSpec(
            num_scalar_prefetch=1,
            grid=(pairs // step_pairs,),
            in_specs=[act_block(kind) for kind in kinds]
            + [pl.BlockSpec((2 * step_pairs, width, hidden), lambda i, core: (i, 0, 0))] * total
            + [whole((rows, LANES))] * len(extra),
            out_specs=[whole(out_dims)] * 2,
            scratch_shapes=[pltpu.VMEM((rows, width), jnp.float32)],
        ),
        out_shape=[jax.ShapeDtypeStruct(out_dims, jnp.bfloat16)] * 2,
        name="expert_rows",
        compiler_params=params(1),
    )(core, *([acts] * total), *weights, *extra)


def middle_back(
    d_kept, d_arrived, probs, share_row, live_lanes, residual, cotangent_rows, gain_row, weight
):
    tokens, width = residual.shape

    def kernel(
        kept_ref,
        arrived_ref,
        prob_ref,
        share_ref,
        live_ref,
        residual_ref,
        cotan_ref,
        gain_ref,
        weight_ref,
        d_residual,
        d_branch,
        d_logits,
        d_gain,
        d_groups,
    ):
        packed = kept_ref[...].astype(jnp.float32) + arrived_ref[...].astype(jnp.float32)
        prob = prob_ref[...]
        live = live_ref[...]
        d_prob = packed[:, width:] + share_ref[...] * live
        logits = (prob * (d_prob - jnp.sum(prob * d_prob, -1, keepdims=True))).astype(jnp.bfloat16)
        d_logits[...] = logits
        d_normed = packed[:, :width] + turned(logits, weight_ref[:, width:])
        total = residual_ref[...]
        scale = rms_scale(total)
        unit = total * scale
        d_gain[...] = jnp.broadcast_to(jnp.sum(d_normed * unit, 0, keepdims=True), (8, width))
        d_unit = d_normed * gain_ref[...]
        d_total = cotan_ref[...].astype(jnp.float32) * live[:, :1] + scale * (
            d_unit - unit * jnp.mean(d_unit * unit, -1, keepdims=True)
        )
        d_residual[...] = d_total
        low = d_total.astype(jnp.bfloat16)
        d_branch[...] = low
        for j in range(KEY_VALUE_HEADS):
            d_groups[j] = turned(
                low, weight_ref[j * QUERY_GROUP : (j + 1) * QUERY_GROUP, :width]
            ).astype(jnp.bfloat16)

    inputs = (d_kept, d_arrived, probs, share_row, live_lanes, residual, cotangent_rows, gain_row, weight)
    out_shape = [
        jax.ShapeDtypeStruct((tokens, width), jnp.float32),
        jax.ShapeDtypeStruct((tokens, width), jnp.bfloat16),
        jax.ShapeDtypeStruct((tokens, LANES), jnp.bfloat16),
        jax.ShapeDtypeStruct((8, width), jnp.float32),
        jax.ShapeDtypeStruct((KEY_VALUE_HEADS, tokens, QUERY_GROUP), jnp.bfloat16),
    ]
    return pl.pallas_call(
        kernel,
        grid=(1,),
        in_specs=[whole(value.shape) for value in inputs],
        out_specs=[whole(value.shape) for value in out_shape],
        out_shape=out_shape,
        name="middle_back",
        compiler_params=params(1),
    )(*inputs)


def early_grads(attended, d_branch, normed, d_logits, d_gain, gain_lane):
    tokens, width = normed.shape
    block = width // 3

    def kernel(attended_ref, branch_ref, normed_ref, logits_ref, gain_ref, out_ref):
        out_ref[:, :width] = over_rows(attended_ref[...], branch_ref[...]).astype(jnp.bfloat16)
        side_term = over_rows(normed_ref[...], logits_ref[...])
        column = jnp.broadcast_to(gain_ref[:1, :], (LANES, block)).T
        lane = lax.broadcasted_iota(jnp.int32, (block, LANES), 1)
        out_ref[:, width:] = jnp.where(lane == gain_lane, column, side_term).astype(jnp.bfloat16)

    return pl.pallas_call(
        kernel,
        grid=(3,),
        in_specs=[
            pl.BlockSpec((tokens, block), lambda i: (0, i)),
            whole((tokens, width)),
            pl.BlockSpec((tokens, block), lambda i: (0, i)),
            whole((tokens, LANES)),
            pl.BlockSpec((8, block), lambda i: (0, i)),
        ],
        out_specs=pl.BlockSpec((block, width + LANES), lambda i: (i, 0)),
        out_shape=jax.ShapeDtypeStruct((width, width + LANES), jnp.bfloat16),
        name="early_grads",
        compiler_params=params(1),
    )(attended, d_branch, normed, d_logits, d_gain)


def project_back(d_fused, fused_weight, normed, rows_in, gain_row, d_residual):
    tokens, width = rows_in.shape
    steps = KEY_VALUE_HEADS // 2
    query_step, head_step = 2 * QUERY_GROUP, 2 * HEAD_DIM
    key_start = KEY_VALUE_HEADS * QUERY_GROUP
    value_start = key_start + KEY_VALUE_HEADS * HEAD_DIM

    def kernel(
        d_ref, query_w, key_w, value_w, normed_ref, rows, gain, d_residual_ref, late, d_input, keep
    ):
        step = pl.program_id(0)
        first, second = d_ref[0], d_ref[1]
        key_end = QUERY_GROUP + HEAD_DIM
        d_pair = jnp.concatenate(
            [
                first[:, :QUERY_GROUP],
                second[:, :QUERY_GROUP],
                first[:, QUERY_GROUP:key_end],
                second[:, QUERY_GROUP:key_end],
                first[:, key_end:],
                second[:, key_end:],
            ],
            1,
        )
        grad = over_rows(normed_ref[...], d_pair).astype(jnp.bfloat16)
        late[:, pl.ds(pl.multiple_of(step * query_step, LANES), query_step)] = grad[:, :query_step]
        late[:, pl.ds(pl.multiple_of(key_start + step * head_step, LANES), head_step)] = grad[
            :, query_step : query_step + head_step
        ]
        late[:, pl.ds(pl.multiple_of(value_start + step * head_step, LANES), head_step)] = grad[
            :, query_step + head_step :
        ]
        term = turned(d_pair, jnp.concatenate([query_w[...], key_w[...], value_w[...]], 1))

        @pl.when(step == 0)
        def _():
            keep[...] = term

        @pl.when(step > 0)
        def _():
            keep[...] += term

        @pl.when(step == steps - 1)
        def _():
            values = rows[...].astype(jnp.float32)
            scale = rms_scale(values)
            unit = values * scale
            d_normed = keep[...]
            d_unit = d_normed * gain[...]
            d_input[...] = d_residual_ref[...] + scale * (
                d_unit - unit * jnp.mean(d_unit * unit, -1, keepdims=True)
            )
            d_gain = jnp.sum(d_normed * unit, 0, keepdims=True)
            late[:, FUSED_WIDTH:] = jnp.broadcast_to(d_gain, (LANES, width)).T.astype(jnp.bfloat16)

    return pl.pallas_call(
        kernel,
        grid=(steps,),
        in_specs=[
            pl.BlockSpec((2, tokens, FUSED_GROUP), lambda i: (i, 0, 0)),
            pl.BlockSpec((width, query_step), lambda i: (0, i)),
            pl.BlockSpec((width, head_step), lambda i: (0, key_start // head_step + i)),
            pl.BlockSpec((width, head_step), lambda i: (0, value_start // head_step + i)),
            whole((tokens, width)),
            whole((tokens, width)),
            whole((1, width)),
            whole((tokens, width)),
        ],
        out_specs=[whole((width, FUSED_WIDTH + LANES)), whole((tokens, width))],
        out_shape=[
            jax.ShapeDtypeStruct((width, FUSED_WIDTH + LANES), jnp.bfloat16),
            jax.ShapeDtypeStruct((tokens, width), jnp.float32),
        ],
        scratch_shapes=[pltpu.VMEM((tokens, width), jnp.float32)],
        name="project_back",
        compiler_params=params(1),
    )(d_fused, fused_weight, fused_weight, fused_weight, normed, rows_in, gain_row, d_residual)


def body(
    layer_input,
    gain_attn,
    w_query,
    key_projection_weight,
    value_projection_weight,
    w_out,
    gain_ffn,
    w_router,
    w_gate,
    w_up,
    w_down,
    routes,
    lengths,
    cotangent,
):
    ctx_parts = lax.axis_size("z")
    n_ctx = 2 * ctx_parts
    n_shard = 2 * lax.axis_size("x")
    ctx_side = lax.axis_index("y")
    ctx_pos = 2 * lax.axis_index("z") + ctx_side
    shard_pos = 2 * lax.axis_index("x") + lax.axis_index("k")
    local_sequences = layer_input.shape[0]
    half_rows = layer_input.shape[3]
    model_width = layer_input.shape[4]
    sequence_rows = 2 * half_rows
    tokens = local_sequences * sequence_rows
    seq_len = n_ctx * sequence_rows
    experts = w_gate.shape[0]
    top_k = routes.shape[4]
    gathered_rows = n_shard * tokens
    head_shares = n_ctx // KEY_VALUE_HEADS
    here_sequences = local_sequences // head_shares
    width_rows = gain_attn.shape[0]

    core_pos = lax.axis_index("k")
    chip_pos = lax.axis_index("x")
    swap = [(0, 1), (1, 0)]

    def added(first, second):
        return (first.astype(jnp.float32) + second.astype(jnp.float32)).astype(jnp.bfloat16)

    def picked(values, which):
        return lax.dynamic_index_in_dim(values, which, 0, keepdims=False)

    def chip_halves(stay, arrived):
        leave_now = added(picked(stay, 1 - chip_pos), picked(arrived, 1 - chip_pos))
        return (
            added(picked(stay, chip_pos), picked(arrived, chip_pos)),
            lax.ppermute(leave_now, "x", swap),
        )

    def halved_by(values, axis_name, which):
        return added(
            picked(values, which), lax.ppermute(picked(values, 1 - which), axis_name, swap)
        )

    def chip_reduced(terms):
        parts = terms.reshape(ctx_parts, 2, 2, 2, -1, terms.shape[1])
        for axis_name, which, dim in (("k", core_pos, 3), ("x", chip_pos, 2)):
            parts = halved_by(jnp.moveaxis(parts, dim, 0), axis_name, which)
        return parts

    def side_reduced(parts):
        parts = halved_by(jnp.moveaxis(parts, 1, 0), "y", ctx_side)
        own = lax.psum_scatter(
            parts.reshape(-1, parts.shape[-1]), "z", scatter_dimension=0, tiled=True
        )
        return own.astype(jnp.float32)

    fused_weight = lax.all_gather(
        jnp.concatenate(
            [
                w_query,
                key_projection_weight,
                value_projection_weight,
                jnp.pad(gain_attn[:, None], ((0, 0), (0, LANES - 1))),
            ],
            1,
        ),
        SHARD,
        axis=0,
        tiled=True,
    )
    out_weight = lax.all_gather(
        jnp.concatenate(
            [
                w_out,
                w_router,
                gain_ffn[:, None],
                jnp.zeros((width_rows, LANES - experts - 1), jnp.bfloat16),
            ],
            1,
        ),
        SHARD,
        axis=0,
        tiled=True,
    )
    gain_one = fused_weight[:, FUSED_WIDTH].astype(jnp.float32)[None, :]
    gain_two = out_weight[:, model_width + experts].astype(jnp.float32)[None, :]
    router_matrix = out_weight[:, model_width : model_width + experts]

    slots = jnp.arange(seq_len, dtype=jnp.int32)
    slot_ctx, slot_row = slots // sequence_rows, slots % sequence_rows
    all_positions = (
        jnp.where(slot_row < half_rows, slot_ctx, 2 * n_ctx - 1 - slot_ctx) * half_rows
        + slot_row % half_rows
    )
    local_positions = lax.dynamic_slice_in_dim(all_positions, ctx_pos * sequence_rows, sequence_rows)
    seq_lengths = lax.dynamic_slice_in_dim(lengths, shard_pos * local_sequences, local_sequences)
    lengths_here = lax.dynamic_slice_in_dim(
        seq_lengths, (ctx_pos % head_shares) * here_sequences, here_sequences
    )
    live_rows = (local_positions[None, :] < seq_lengths[:, None]).reshape(tokens)
    live_lanes = jnp.broadcast_to(live_rows.astype(jnp.float32)[:, None], (tokens, LANES))
    live_group = (
        (local_positions[None, :] < lengths[:, None]).astype(jnp.float32).reshape(gathered_rows)
    )
    row_positions = jnp.broadcast_to(all_positions[:, None], (seq_len, LANES))
    column_positions = jnp.broadcast_to(all_positions[None, :], (8, seq_len))
    every_cos, every_sin = rope_tables(all_positions)
    own_cos, own_sin = rope_tables(local_positions)
    step_cos = jnp.tile(own_cos, (local_sequences, 2 * (GROUP + 1)))
    step_sin = jnp.tile(own_sin, (local_sequences, 2 * (GROUP + 1)))
    pair_cos, pair_sin = jnp.tile(every_cos, (1, 2)), jnp.tile(every_sin, (1, 2))

    rows_in = layer_input.reshape(tokens, model_width)
    cotangent_rows = cotangent.reshape(tokens, model_width)
    d_moe = jnp.where(live_rows[:, None], cotangent_rows, jnp.bfloat16(0.0))
    d_moe_all = lax.all_gather(d_moe, SHARD, axis=0, tiled=True)
    d_moe_turned = d_moe_all.T

    def exchange(groups):
        return lax.all_to_all(groups, CTX, 0, 0, tiled=True)

    fused_own, first_normed = project_in(rows_in, gain_one, fused_weight, step_cos, step_sin)
    fused_rows = exchange(
        fused_own.reshape(n_ctx, here_sequences, sequence_rows, FUSED_GROUP)
    )
    attended_rows = attend(fused_rows, row_positions, column_positions, lengths_here)
    attended_groups = exchange(attended_rows).reshape(KEY_VALUE_HEADS, tokens, QUERY_GROUP)
    residual, second_normed, attended_low = project_out(
        attended_groups, rows_in, out_weight, gain_two
    )

    normed_all = lax.all_gather(second_normed, SHARD, axis=0, tiled=True)
    normed_turned = normed_all.T
    router_probs = jax.nn.softmax(plain(normed_all, router_matrix), axis=-1)
    route_hot = jnp.any(
        routes.reshape(gathered_rows, top_k, 1) == jnp.arange(experts, dtype=jnp.int32), axis=1
    ).astype(jnp.float32)
    lane_pad = ((0, 0), (0, LANES - experts))
    prob_table = jnp.pad(router_probs, lane_pad)
    hot_table = jnp.pad(route_hot, lane_pad)
    gate_table = prob_table * hot_table

    group_sums = jnp.concatenate(
        [
            jnp.sum(hot_table * live_group[:, None], 0, keepdims=True),
            jnp.sum(prob_table * live_group[:, None], 0, keepdims=True),
        ],
        0,
    )
    sum_steps = [("y", 1)]
    while 2 ** (len(sum_steps) - 1) < ctx_parts:
        sum_steps.append(("z", 2 ** (len(sum_steps) - 1)))

    def summed_once(values, axis_name, step):
        count = lax.axis_size(axis_name)
        return values + lax.ppermute(values, axis_name, [(i, i ^ step) for i in range(count)])


    side = ctx_side.astype(jnp.int32).reshape(1)
    core = core_pos.astype(jnp.int32).reshape(1)
    acts, d_gates, reduced = None, None, []
    first_expert = 0
    for number, chunk in enumerate(CHUNKS):
        if 0 < number <= len(sum_steps):
            group_sums = summed_once(group_sums, *sum_steps[number - 1])
            acts, group_sums = lax.optimization_barrier((acts, group_sums))
        *terms, acts, gate_piece = expert_chunk(
            first_expert,
            chunk,
            side,
            ctx_parts,
            normed_all,
            normed_turned,
            d_moe_all,
            d_moe_turned,
            gate_table,
            w_gate,
            w_up,
            w_down,
            acts,
            number > 0,
        )
        first_expert += chunk
        d_gates = gate_piece if d_gates is None else d_gates + gate_piece
        if number:
            arrived = lax.ppermute(terms[1], "y", swap)
            halved = added(terms[0], arrived)
            if number == 1:
                first_halved = halved
            if number == 2:
                second_halved = halved
            reduced.append(lax.psum_scatter(halved, "z", scatter_dimension=2, tiled=True))
        else:
            ringed = lax.psum_scatter(terms[0], "z", scatter_dimension=2, tiled=True)

    for sum_step in sum_steps[len(CHUNKS) - 1 :]:
        group_sums = summed_once(group_sums, *sum_step)
    all_sums = group_sums[:, :experts]

    acts, first_halved = lax.optimization_barrier((acts, first_halved))
    d_stay, d_leave = expert_rows(core, (1, 2), (w_gate, w_up), acts, d_gates, hot_table)
    d_came = lax.ppermute(d_leave, "k", swap)
    d_kept, d_arrived = chip_halves(d_stay, d_came)
    moe_stay, moe_leave = expert_rows(core, (0,), (w_down,), acts, None, None)
    moe_kept, moe_arrived = chip_halves(moe_stay, lax.ppermute(moe_leave, "k", swap))
    layer_output = (
        (residual + moe_kept.astype(jnp.float32) + moe_arrived.astype(jnp.float32))
        .astype(jnp.bfloat16)
        .reshape(layer_input.shape)
    )
    ringed = jnp.moveaxis(
        ringed.reshape(3, CHUNKS[0], 2, model_width // n_ctx, -1), 2, 0
    )
    reduced.insert(0, halved_by(ringed, "y", ctx_side))

    live_all = jnp.sum(lengths).astype(jnp.float32)
    route_share = all_sums[0] / (top_k * live_all)
    aux_loss = experts * jnp.sum(route_share * all_sums[1] / live_all)
    share_row = jnp.pad((loss_weight * experts / live_all) * route_share[None, :], lane_pad)

    own_probs = lax.dynamic_slice_in_dim(prob_table, shard_pos * tokens, tokens, 0)
    d_residual, d_branch, d_logits, d_gain_two, d_groups = middle_back(
        d_kept,
        d_arrived,
        own_probs,
        share_row,
        live_lanes,
        residual,
        cotangent_rows,
        gain_two,
        out_weight,
    )
    d_attended = exchange(d_groups.reshape(n_ctx, here_sequences, sequence_rows, QUERY_GROUP))
    d_branch, d_attended, second_halved = lax.optimization_barrier(
        (d_branch, d_attended, second_halved)
    )
    early_terms = early_grads(attended_low, d_branch, second_normed, d_logits, d_gain_two, experts)
    early_parts = chip_reduced(early_terms)
    d_fused_rows = attend_back(
        fused_rows,
        d_attended,
        row_positions,
        column_positions,
        pair_cos,
        pair_sin,
        lengths_here,
    )
    d_fused = exchange(d_fused_rows)
    d_fused = d_fused.reshape(KEY_VALUE_HEADS, tokens, FUSED_GROUP)
    late_terms, grad_input = project_back(
        d_fused, fused_weight, first_normed, rows_in, gain_one, d_residual
    )
    early_parts, late_terms = lax.optimization_barrier((early_parts, late_terms))
    early_rows = side_reduced(early_parts)
    late_rows = side_reduced(chip_reduced(late_terms))
    query_end = KEY_VALUE_HEADS * QUERY_GROUP
    key_end = query_end + KEY_VALUE_HEADS * HEAD_DIM
    grads = [
        jnp.concatenate([piece[kind] for piece in reduced], 0).astype(jnp.float32)
        for kind in range(3)
    ]
    return (
        layer_output,
        grad_input.reshape(layer_input.shape),
        late_rows[:, FUSED_WIDTH],
        late_rows[:, :query_end],
        late_rows[:, query_end:key_end],
        late_rows[:, key_end:FUSED_WIDTH],
        early_rows[:, :model_width],
        early_rows[:, model_width + experts],
        early_rows[:, model_width : model_width + experts],
        grads[0],
        grads[1],
        grads[2],
        aux_loss,
    )


def solution(mesh):
    n_ctx, n_shard = mesh.shape["ctx"], mesh.shape["fsdp"]
    fine = Mesh(mesh.devices.reshape(n_ctx // 2, 2, n_shard // 2, 2), EVERY)
    placed = (
        P(SHARD, CTX, None, None, None),
        P(SHARD),
        P(SHARD, None),
        P(SHARD, None),
        P(SHARD, None),
        P(SHARD, None),
        P(SHARD),
        P(SHARD, None),
        P(None, None, SHARD),
        P(None, None, SHARD),
        P(None, None, SHARD),
        P(None, CTX, None, None, None),
        P(),
        P(SHARD, CTX, None, None, None),
    )
    return jax.shard_map(
        body,
        mesh=fine,
        in_specs=placed,
        out_specs=(
            P(SHARD, CTX, None, None, None),
            P(SHARD, CTX, None, None, None),
            P(EVERY),
            P(EVERY, None),
            P(EVERY, None),
            P(EVERY, None),
            P(EVERY, None),
            P(EVERY),
            P(EVERY, None),
            P(None, CTX, SHARD),
            P(None, CTX, SHARD),
            P(None, CTX, SHARD),
            P(),
        ),
        check_vma=False,
    )
```
